128 devices in a mesh: row: 16 (over z, y_hi, core), col: 4 (over x), depth: 2 (over y_lo).
Axes of the slice: x: 4, y: 4 (y_hi: 2, y_lo: 2; y = y_hi * 2 + y_lo), z: 4, core: 2. Of those that a mesh axis runs over, the one named last changes fastest.
Arguments:
- left_block: bfloat16 [4, 32768, 512], P(None, ('row', 'depth'), 'col'), may hold values from -6 to 6
- right_block: bfloat16 [512, 2, 16384], P(('row', 'depth'), None, 'col'), may hold values from -0.125 to 0.125
- slice_ids: int32 [4], replicated, may hold values from 0 to 1, as said below
- mode_order: int32 [9], replicated, may hold values from 0 to 8, each once
Outputs:
- contracted: float32 [32768, 16384], P(('row', 'depth'), 'col')
The draws below stay inside these ranges and needn't reach their ends.
Inputs may be any that keep to these rules, and one draw needn't show every extreme that they name: mode_order holds every number of 0 to 8 once. `slice_ids`: each value of the sliced bond is taken by exactly 2 slices.
All inputs are finite; a program needn't handle non-finite values.
Results may differ from the reference program's by a relative error of at most 0.0003.
Values may be sent and summed in bfloat16 or wider, within the bound.
A program may use at most 128 MiB of HBM per device.

```python
import jax
import jax.numpy as jnp
from jax import lax

BITS = 9
K = 512
N = 16384
CHOICES = 2
SLICES = 4
M = 32768


def draw_slice_ids(key, part):
    order = jax.random.permutation(jax.random.fold_in(key, 17), SLICES)
    return (order % CHOICES).astype(jnp.int32)


def shard_levels(rng, shape, pieces, smallest, top_value):
    factor_of, own = 1.0, jax.random.fold_in(rng, 6)
    for dim, parts in pieces:
        steps = jnp.exp(jax.random.uniform(jax.random.fold_in(own, dim), (parts,), jnp.float32, smallest / len(pieces), top_value / len(pieces)))
        factor_of = factor_of * jnp.repeat(steps, shape[dim] // parts).reshape([-1 if axis == dim else 1 for axis in range(len(shape))])
    return factor_of


def gaussian(rng, shape, scale, bound, pieces=(), held_as=jnp.bfloat16):
    factor_of = shard_levels(rng, shape, pieces, -0.22, 0.18) if pieces else 1.0
    array = jax.random.normal(rng, shape, jnp.float32) * scale * factor_of
    return jnp.minimum(jnp.maximum(array, -bound), bound).astype(held_as)


def setup_inputs(seed: int = 0) -> dict:
    arg_keys = jax.random.split(jax.random.key(seed), 5)
    left_block = gaussian(arg_keys[0], (SLICES, M, K), 1.0, 6.0, ((1, 32), (2, 4)))
    right_block = gaussian(arg_keys[1], (K, CHOICES, N), (SLICES * K) ** -0.5, 0.125, ((0, 32), (2, 4)))
    slice_ids = draw_slice_ids(jax.random.fold_in(arg_keys[4], 71), 0)
    mode_order = jax.random.permutation(arg_keys[3], BITS).astype(jnp.int32)
    return dict(left_block=left_block, right_block=right_block, slice_ids=slice_ids, mode_order=mode_order)


def stored_order(mode_order, columns):
    logical = jnp.arange(columns, dtype=jnp.int32)
    stored = jnp.zeros((columns,), jnp.int32)
    for bit_place in range(mode_order.shape[0]):
        stored = stored + ((logical // (2 ** bit_place)) % 2) * jnp.left_shift(jnp.int32(1), mode_order[bit_place].astype(jnp.int32))
    return stored.astype(jnp.int32)


def reference(left_block, right_block, slice_ids, mode_order):
    ordered = jnp.take(left_block, stored_order(mode_order, left_block.shape[2]), axis=2)
    total = jnp.zeros((left_block.shape[1], right_block.shape[2]), jnp.float32)
    for number in range(left_block.shape[0]):
        partner = lax.dynamic_index_in_dim(right_block, slice_ids[number].astype(jnp.int32), 1, keepdims=False)
        total = total + jnp.dot(ordered[number].astype(jnp.float32), partner.astype(jnp.float32), preferred_element_type=jnp.float32)
    return total
```

```python
import functools
import math

import jax
import jax.numpy as jnp
import numpy as np
from jax import lax
from jax.experimental import pallas as pl
from jax.experimental.pallas import tpu as pltpu
from jax.sharding import PartitionSpec as P

MESH = pl.DeviceIdType.MESH
CHUNKS = 8
EARLY = 7
CODE_TOP = 32000.0
STEPS_PER_OCTAVE = 16.0
LN2 = math.log(2.0)


def tile_product(a_ref, b_ref, i, j, width):
    cols = pl.ds(pl.multiple_of(j * width, width), width)
    b = b_ref[:, :, :, :, :, cols]
    b = b.reshape(-1, width)
    both = jnp.dot(a_ref[i], b, preferred_element_type=jnp.float32)
    rows = both.shape[0] // 2
    return both[:rows] + both[rows:]


def gather_kernel(
    ids_ref,
    order_ref,
    left_ref,
    right_ref,
    a_ref,
    b_ref,
    part_ref,
    code,
    pick,
    send1,
    recv1,
    send,
    recv,
):
    slices, rows_all, part_k = left_ref.shape
    values, shard_k, columns = right_ref.shape
    rows, width = rows_all // CHUNKS, columns // CHUNKS
    bond = 4 * part_k

    row, c, y_lo = lax.axis_index("row"), lax.axis_index("col"), lax.axis_index("depth")
    core = row % 2
    y = (row // 2) % 2 * 2 + y_lo
    z = row // 4
    p1 = y * (1 - core) + z * core
    p2 = z * (1 - core) + y * core

    def place(y_at, z_at, core_at):
        return ((z_at * 2 + y_at // 2) * 2 + core_at, c, y_at % 2)

    def first(d):
        return place((y + (1 - core) * d) % 4, (z + core * d) % 4, core)

    def second(d):
        return place((y + core * d) % 4, (z + (1 - core) * d) % 4, core)

    def along(d):
        return (row, (c + d) % 4, y_lo)

    sibling = place(y, z, 1 - core)

    barrier = pltpu.get_barrier_semaphore()
    for other in (first(1), first(3), second(1), second(3), along(1), along(3), sibling):
        pl.semaphore_signal(barrier, inc=1, device_id=other, device_id_type=MESH)

    own = b_ref.at[:, core, p2, p1]
    own[...] = right_ref[...]

    def copy(ref, sems, at, device):
        return pltpu.make_async_remote_copy(
            src_ref=ref,
            dst_ref=ref,
            send_sem=sems[0].at[at],
            recv_sem=sems[1].at[at],
            device_id=device,
            device_id_type=MESH,
        )

    once, many = (send1, recv1), (send, recv)
    left1, right1, far1 = (p1 + 3) % 4, (p1 + 1) % 4, (p1 + 2) % 4

    def phase1(kind):
        if kind == 0:
            return copy(own, once, 0, first(1)), b_ref.at[:, core, p2, left1]
        if kind == 1:
            return copy(own, once, 1, first(3)), b_ref.at[:, core, p2, right1]
        if kind == 2:
            return copy(b_ref.at[0, core, p2, left1], once, 2, first(1)), b_ref.at[0, core, p2, far1]
        return copy(b_ref.at[1, core, p2, right1], once, 3, first(3)), b_ref.at[1, core, p2, far1]

    def start1(kind):
        phase1(kind)[0].start()

    def arrived1(kind):
        copy(phase1(kind)[1], once, kind, sibling).wait_recv()

    def sent1(kind):
        phase1(kind)[0].wait_send()

    left2, right2, far2 = (p2 + 3) % 4, (p2 + 1) % 4, (p2 + 2) % 4

    def moved(kind, t):
        cols = pl.ds(pl.multiple_of(t * width, width), width)

        def group(plane, p):
            return b_ref.at[:, plane, p, :, :, cols]

        def half(v, p):
            return b_ref.at[v, core, p, :, :, cols]

        if kind == 0:
            return group(core, p2), second(1), group(core, left2)
        if kind == 1:
            return group(core, p2), second(3), group(core, right2)
        if kind == 2:
            return half(0, left2), second(1), half(0, far2)
        if kind == 3:
            return half(1, right2), second(3), half(1, far2)
        if kind == 4:
            return group(core, p2), sibling, group(1 - core, p1)
        if kind == 5:
            return group(core, left2), sibling, group(1 - core, left1)
        if kind == 6:
            return group(core, right2), sibling, group(1 - core, right1)
        if kind == 7:
            return group(core, far2), sibling, group(1 - core, far1)
        if kind == 8:
            return code.at[t, c], along(1), code.at[t, (c + 3) % 4]
        if kind == 9:
            return code.at[t, c], along(3), code.at[t, (c + 1) % 4]
        if kind == 10:
            return code.at[t, (c + 3) % 4, 0], along(1), code.at[t, (c + 2) % 4, 0]
        return code.at[t, (c + 1) % 4, 1], along(3), code.at[t, (c + 2) % 4, 1]

    def start(kind, t):
        ref, device, _ = moved(kind, t)
        copy(ref, many, (kind, t), device).start()

    def arrived(kind, t):
        copy(moved(kind, t)[2], many, (kind, t), sibling).wait_recv()

    def sent(kind, t):
        ref, device, _ = moved(kind, t)
        copy(ref, many, (kind, t), device).wait_send()

    pl.semaphore_wait(barrier, 7)
    start1(0)
    start1(1)

    weights = [
        [jnp.where(ids_ref[s] == v, 1.0, 0.0).astype(jnp.float32) for s in range(slices)]
        for v in range(values)
    ]

    def encode(t, carry):
        here = pl.ds(pl.multiple_of(t * rows, rows), rows)
        blocks = [left_ref[s, here, :].astype(jnp.float32) for s in range(slices)]
        for v in range(values):
            total = blocks[0] * weights[v][0]
            for s in range(1, slices):
                total = total + blocks[s] * weights[v][s]
            top = jnp.max(jnp.abs(total), axis=0, keepdims=True)
            top = jnp.maximum(top, 2.0**-110)
            level = jnp.ceil(jnp.log(top) * (STEPS_PER_OCTAVE / LN2))
            scale = jnp.exp(level * (-LN2 / STEPS_PER_OCTAVE)) * CODE_TOP
            code[t, c, v, :rows, :] = jnp.round(total * scale).astype(jnp.int32).astype(jnp.int16)
            code[t, c, v, rows:, :] = jnp.broadcast_to(level, (16, part_k)).astype(jnp.int32).astype(jnp.int16)
        start(8, t)
        start(9, t)
        return carry

    lax.fori_loop(0, CHUNKS, encode, 0)

    place_at = lax.broadcasted_iota(jnp.int32, (bond, bond), 1)
    j = place_at & 15
    q1, q2, plane = (place_at >> 4) & 3, (place_at >> 6) & 3, place_at >> 8
    at_y = q1 * (1 - plane) + q2 * plane
    at_z = q2 * (1 - plane) + q1 * plane
    shard = at_z * 8 + (at_y >> 1) * 4 + plane * 2 + (at_y & 1)
    logical = shard * shard_k + j
    stored = jnp.zeros((bond, bond), jnp.int32)
    for bit in range(order_ref.shape[0]):
        stored = stored + ((logical >> bit) & 1) * jnp.left_shift(jnp.int32(1), order_ref[bit])
    hit = lax.broadcasted_iota(jnp.int32, (bond, bond), 0) == stored
    pick[...] = jnp.where(hit, 1.0, 0.0).astype(jnp.bfloat16)

    arrived1(0)
    start1(2)
    arrived1(1)
    start1(3)
    arrived1(2)
    arrived1(3)

    def lead(t):
        for kind in (0, 1, 4):
            start(kind, t)

    lead(0)
    lead(1)

    def decode(t):
        parts = []
        for v in range(values):
            high, low = [], []
            for at in range(4):
                level = code[t, at, v, rows:, :].astype(jnp.int32).astype(jnp.float32)[:1]
                scale = jnp.exp(level * (LN2 / STEPS_PER_OCTAVE)) * (1.0 / CODE_TOP)
                x = code[t, at, v, :rows, :].astype(jnp.int32).astype(jnp.float32) * scale
                h = x.astype(jnp.bfloat16)
                high.append(h)
                low.append((x - h.astype(jnp.float32)).astype(jnp.bfloat16))
            parts += [jnp.concatenate(high, axis=1), jnp.concatenate(low, axis=1)]
        picked = jnp.dot(
            jnp.concatenate(parts, axis=0), pick[...], preferred_element_type=jnp.float32
        ).astype(jnp.bfloat16)
        for v in range(values):
            a_ref[t, :, v * bond : (v + 1) * bond] = picked[2 * rows * v : 2 * rows * (v + 1)]

    def tile(i, j):
        here = pl.ds(pl.multiple_of(i * rows, rows), rows)
        cols = pl.ds(pl.multiple_of(j * width, width), width)
        part_ref[here, cols] = tile_product(a_ref, b_ref, i, j, width)

    def tick(t, carry):
        @pl.when(t < CHUNKS)
        def _():
            arrived(8, t)
            start(10, t)
            arrived(9, t)
            start(11, t)
            arrived(0, t)
            start(2, t)
            start(5, t)
            arrived(1, t)
            start(3, t)
            start(6, t)

        @pl.when(t < CHUNKS - 2)
        def _():
            lead(t + 2)

        @pl.when((t >= 1) & (t < CHUNKS + 1))
        def _():
            arrived(2, t - 1)
            arrived(3, t - 1)
            start(7, t - 1)
            arrived(10, t - 1)
            arrived(11, t - 1)
            decode(t - 1)

        @pl.when(t >= 2)
        def _():
            for kind in (4, 5, 6, 7):
                arrived(kind, t - 2)

        @pl.when((t >= 2) & (t < EARLY + 2))
        def _():
            u = t - 2

            def across(q, carry):
                tile(u, q)
                return carry

            def down(q, carry):
                tile(q, u)
                return carry

            lax.fori_loop(0, u, across, 0)
            lax.fori_loop(0, u + 1, down, 0)

        return carry

    lax.fori_loop(0, CHUNKS + 2, tick, 0)

    for kind in range(4):
        sent1(kind)

    def settle(t, carry):
        for kind in range(12):
            sent(kind, t)
        return carry

    lax.fori_loop(0, CHUNKS, settle, 0)


def finish_kernel(a_ref, b_ref, part_ref, out_ref, last, sems):
    rows, width = last.shape[1], last.shape[2]
    early = part_ref.shape
    done = pltpu.make_async_copy(
        part_ref, out_ref.at[: early[0], : early[1]], sems.at[2 * CHUNKS - 1]
    )
    done.start()
    u = CHUNKS - 1

    def out_copy(q, i, j):
        here = pl.ds(pl.multiple_of(i * rows, rows), rows)
        cols = pl.ds(pl.multiple_of(j * width, width), width)
        return pltpu.make_async_copy(last.at[q], out_ref.at[here, cols], sems.at[q])

    def across(q, carry):
        last[q] = tile_product(a_ref, b_ref, u, q, width)
        out_copy(q, u, q).start()
        return carry

    def down(q, carry):
        last[u + q] = tile_product(a_ref, b_ref, q, u, width)
        out_copy(u + q, q, u).start()
        return carry

    lax.fori_loop(0, u, across, 0)
    lax.fori_loop(0, u + 1, down, 0)

    def across_wait(q, carry):
        out_copy(q, u, q).wait()
        return carry

    def down_wait(q, carry):
        out_copy(u + q, q, u).wait()
        return carry

    lax.fori_loop(0, u, across_wait, 0)
    lax.fori_loop(0, u + 1, down_wait, 0)
    done.wait()


def per_device(left_block, right_block, slice_ids, mode_order):
    slices, rows_all, part_k = left_block.shape
    shard_k, values, columns = right_block.shape
    rows, width = rows_all // CHUNKS, columns // CHUNKS
    bond = 4 * part_k
    right = jnp.transpose(right_block, (1, 0, 2))
    vmem = pl.BlockSpec(memory_space=pltpu.VMEM)
    smem = pl.BlockSpec(memory_space=pltpu.SMEM)
    a, b, part = pl.pallas_call(
        gather_kernel,
        out_shape=(
            pltpu.VMEM((CHUNKS, 2 * rows, values * bond), jnp.bfloat16),
            pltpu.VMEM((values, 2, 4, 4, shard_k, columns), jnp.bfloat16),
            pltpu.VMEM((EARLY * rows, EARLY * width), jnp.float32),
        ),
        in_specs=[smem, smem, vmem, vmem],
        out_specs=(vmem, vmem, vmem),
        scratch_shapes=[
            pltpu.VMEM((CHUNKS, 4, values, rows + 16, part_k), jnp.int16),
            pltpu.VMEM((bond, bond), jnp.bfloat16),
            pltpu.SemaphoreType.DMA((4,)),
            pltpu.SemaphoreType.DMA((4,)),
            pltpu.SemaphoreType.DMA((12, CHUNKS)),
            pltpu.SemaphoreType.DMA((12, CHUNKS)),
        ],
        compiler_params=pltpu.CompilerParams(
            collective_id=0, has_side_effects=True, vmem_limit_bytes=16 << 20
        ),
    )(slice_ids, mode_order, left_block, right)
    return pl.pallas_call(
        finish_kernel,
        out_shape=jax.ShapeDtypeStruct((rows_all, columns), jnp.float32),
        in_specs=[vmem, vmem, vmem],
        out_specs=pl.BlockSpec(memory_space=pl.ANY),
        scratch_shapes=[
            pltpu.VMEM((2 * CHUNKS - 1, rows, width), jnp.float32),
            pltpu.SemaphoreType.DMA((2 * CHUNKS,)),
        ],
        compiler_params=pltpu.CompilerParams(vmem_limit_bytes=16 << 20),
    )(a, b, part)


def solution(mesh):
    in_specs = (P(None, ("row", "depth"), "col"), P(("row", "depth"), None, "col"), P(), P())
    out_specs = P(("row", "depth"), "col")
    return jax.shard_map(
        per_device, mesh=mesh, in_specs=in_specs, out_specs=out_specs, check_vma=False
    )
```

```python
import functools
import math

import jax
import jax.numpy as jnp
from jax import lax
from jax.experimental import pallas as pl
from jax.experimental.pallas import tpu as pltpu
from jax.sharding import PartitionSpec as P

MESH = pl.DeviceIdType.MESH
ROW_CHUNKS = 4
PAIRS = 4
EARLY = 3
CODE_TOP = 32000.0
STEPS_PER_OCTAVE = 16.0
LN2 = math.log(2.0)


def tile_product(a_ref, b_ref, i, j, width):
    cols = pl.ds(pl.multiple_of(j * width, width), width)
    b = b_ref[:, :, :, :, :, cols]
    b = b.reshape(-1, width)
    both = jnp.dot(a_ref[i], b, preferred_element_type=jnp.float32)
    rows = both.shape[0] // 2
    return both[:rows] + both[rows:]


def gather_kernel(
    ids_hbm,
    order_hbm,
    left_hbm,
    right_ref,
    a_ref,
    b_ref,
    part_ref,
    ids,
    order,
    left,
    code,
    pick,
    local,
    send,
    recv,
    left_send,
    left_recv,
):
    slices, rows_all, part_k = left.shape
    values, shard_k, columns = right_ref.shape
    rows, width = rows_all // ROW_CHUNKS, columns // PAIRS
    strip = width // 2
    bond = 4 * part_k

    row, c, y_lo = lax.axis_index("row"), lax.axis_index("col"), lax.axis_index("depth")
    core = row % 2
    y = (row // 2) % 2 * 2 + y_lo
    z = row // 4

    def place(y_at, z_at, core_at):
        return ((z_at * 2 + y_at // 2) * 2 + core_at, c, y_at % 2)

    def along_y(d):
        return place((y + d) % 4, z, core)

    def along_z(d):
        return place(y, (z + d) % 4, core)

    def along_x(d):
        return (row, (c + d) % 4, y_lo)

    sibling = place(y, z, 1 - core)

    barrier = pltpu.get_barrier_semaphore()
    for other in (along_y(1), along_y(3), along_z(1), along_z(3), along_x(1), along_x(3), sibling):
        pl.semaphore_signal(barrier, inc=1, device_id=other, device_id_type=MESH)

    staged = [
        pltpu.make_async_copy(left_hbm, left, local.at[0]),
        pltpu.make_async_copy(ids_hbm, ids, local.at[1]),
        pltpu.make_async_copy(order_hbm, order, local.at[2]),
    ]
    for one in staged:
        one.start()
    b_ref[:, core, z, y] = right_ref[...]

    def copy(ref, sems, at, device):
        return pltpu.make_async_remote_copy(
            src_ref=ref,
            dst_ref=ref,
            send_sem=sems[0].at[at],
            recv_sem=sems[1].at[at],
            device_id=device,
            device_id_type=MESH,
        )

    many, lefts = (send, recv), (left_send, left_recv)

    def moved(half, kind, p):
        cols = pl.ds(pl.multiple_of(p * width + half * strip, strip), strip)
        first, second = (along_y, along_z) if half == 0 else (along_z, along_y)
        at1, at2 = (y, z) if half == 0 else (z, y)

        def one(v, d):
            at = (at1 + d) % 4
            where = (z, at) if half == 0 else (at, y)
            return b_ref.at[(v, core, *where, slice(None), cols)]

        def group(v, plane, d):
            at = (at2 + d) % 4
            where = (at, slice(None)) if half == 0 else (slice(None), at)
            return b_ref.at[(v, plane, *where, slice(None), cols)]

        both = slice(None)
        if kind == 0:
            return one(both, 0), first(1), one(both, 3)
        if kind == 1:
            return one(both, 0), first(3), one(both, 1)
        if kind == 2:
            return one(0, 3), first(1), one(0, 2)
        if kind == 3:
            return one(1, 1), first(3), one(1, 2)
        if kind == 4:
            return group(both, core, 0), second(1), group(both, core, 3)
        if kind == 5:
            return group(both, core, 0), second(3), group(both, core, 1)
        if kind == 6:
            return group(0, core, 3), second(1), group(0, core, 2)
        if kind == 7:
            return group(1, core, 1), second(3), group(1, core, 2)
        d = (0, 3, 1, 2)[kind - 8]
        return group(both, core, d), sibling, group(both, 1 - core, d)

    def start(half, kind, p):
        ref, device, _ = moved(half, kind, p)
        copy(ref, many, (12 * half + kind, p), device).start()

    def arrived(half, kind, p):
        copy(moved(half, kind, p)[2], many, (12 * half + kind, p), sibling).wait_recv()

    def sent(half, kind, p):
        ref, device, _ = moved(half, kind, p)
        copy(ref, many, (12 * half + kind, p), device).wait_send()

    def left_moved(kind, q):
        before, after, far = (c + 3) % 4, (c + 1) % 4, (c + 2) % 4
        if kind == 0:
            return code.at[q, c], along_x(1), code.at[q, before]
        if kind == 1:
            return code.at[q, c], along_x(3), code.at[q, after]
        if kind == 2:
            return code.at[q, before, 0], along_x(1), code.at[q, far, 0]
        return code.at[q, after, 1], along_x(3), code.at[q, far, 1]

    def left_start(kind, q):
        ref, device, _ = left_moved(kind, q)
        copy(ref, lefts, (kind, q), device).start()

    def left_arrived(kind, q):
        copy(left_moved(kind, q)[2], lefts, (kind, q), sibling).wait_recv()

    def left_sent(kind, q):
        ref, device, _ = left_moved(kind, q)
        copy(ref, lefts, (kind, q), device).wait_send()

    def own_start(p):
        for half in (0, 1):
            start(half, 0, p)
            start(half, 1, p)

    def own_forward(p):
        for half in (0, 1):
            arrived(half, 0, p)
            start(half, 2, p)
            arrived(half, 1, p)
            start(half, 3, p)

    pl.semaphore_wait(barrier, 7)
    own_start(0)
    own_start(1)
    for one in staged:
        one.wait()

    weights = [
        [jnp.where(ids[s] == v, 1.0, 0.0).astype(jnp.float32) for s in range(slices)]
        for v in range(values)
    ]

    def encode(q, carry):
        here = pl.ds(pl.multiple_of(q * rows, rows), rows)
        blocks = [left[s, here, :].astype(jnp.float32) for s in range(slices)]
        for v in range(values):
            total = blocks[0] * weights[v][0]
            for s in range(1, slices):
                total = total + blocks[s] * weights[v][s]
            top = jnp.max(jnp.abs(total), axis=0, keepdims=True)
            top = jnp.maximum(top, 2.0**-110)
            level = jnp.ceil(jnp.log(top) * (STEPS_PER_OCTAVE / LN2))
            scale = jnp.exp(level * (-LN2 / STEPS_PER_OCTAVE)) * CODE_TOP
            code[q, c, v, :rows, :] = jnp.round(total * scale).astype(jnp.int32).astype(jnp.int16)
            code[q, c, v, rows:, :] = jnp.broadcast_to(level, (16, part_k)).astype(jnp.int32).astype(jnp.int16)

        @pl.when(q < 2)
        def _():
            left_start(0, q)
            left_start(1, q)

        return carry

    lax.fori_loop(0, 2, encode, 0)
    own_forward(0)
    lax.fori_loop(2, ROW_CHUNKS, encode, 0)

    place_at = lax.broadcasted_iota(jnp.int32, (8, bond), 1)
    j = place_at & 15
    at_y, at_z, plane = (place_at >> 4) & 3, (place_at >> 6) & 3, place_at >> 8
    shard = at_z * 8 + (at_y >> 1) * 4 + plane * 2 + (at_y & 1)
    logical = shard * shard_k + j
    stored = jnp.zeros((8, bond), jnp.int32)
    for bit in range(order.shape[0]):
        stored = stored + ((logical >> bit) & 1) * jnp.left_shift(jnp.int32(1), order[bit])
    hit = lax.broadcasted_iota(jnp.int32, (bond, bond), 0) == stored[:1]
    pick[...] = jnp.where(hit, 1.0, 0.0).astype(jnp.bfloat16)

    def decode(q):
        parts = []
        for v in range(values):
            high, low = [], []
            for at in range(4):
                level = code[q, at, v, rows:, :].astype(jnp.int32).astype(jnp.float32)[:1]
                scale = jnp.exp(level * (LN2 / STEPS_PER_OCTAVE)) * (1.0 / CODE_TOP)
                x = code[q, at, v, :rows, :].astype(jnp.int32).astype(jnp.float32) * scale
                h = x.astype(jnp.bfloat16)
                high.append(h)
                low.append((x - h.astype(jnp.float32)).astype(jnp.bfloat16))
            parts += [jnp.concatenate(high, axis=1), jnp.concatenate(low, axis=1)]
        picked = jnp.dot(
            jnp.concatenate(parts, axis=0), pick[...], preferred_element_type=jnp.float32
        ).astype(jnp.bfloat16)
        for v in range(values):
            a_ref[q, :, v * bond : (v + 1) * bond] = picked[2 * rows * v : 2 * rows * (v + 1)]

    def tile(q, p):
        here = pl.ds(pl.multiple_of(q * rows, rows), rows)
        cols = pl.ds(pl.multiple_of(p * width, width), width)
        part_ref[here, cols] = tile_product(a_ref, b_ref, q, p, width)

    def turn(u, carry):
        @pl.when(u < PAIRS - 1)
        def _():
            own_forward(u + 1)

        @pl.when(u < PAIRS - 2)
        def _():
            own_start(u + 2)

        @pl.when(u < PAIRS)
        def _():
            for half in (0, 1):
                arrived(half, 2, u)
                arrived(half, 3, u)
                start(half, 4, u)
                start(half, 5, u)
                start(half, 8, u)

        @pl.when(u < ROW_CHUNKS)
        def _():
            left_arrived(0, u)
            left_start(2, u)
            left_arrived(1, u)
            left_start(3, u)

        @pl.when(u < ROW_CHUNKS - 2)
        def _():
            left_start(0, u + 2)
            left_start(1, u + 2)

        @pl.when((u >= 1) & (u < PAIRS + 1))
        def _():
            for half in (0, 1):
                arrived(half, 4, u - 1)
                start(half, 6, u - 1)
                start(half, 9, u - 1)
                arrived(half, 5, u - 1)
                start(half, 7, u - 1)
                start(half, 10, u - 1)

        @pl.when((u >= 1) & (u < ROW_CHUNKS + 1))
        def _():
            left_arrived(2, u - 1)
            left_arrived(3, u - 1)
            decode(u - 1)

        @pl.when((u >= 2) & (u < PAIRS + 2))
        def _():
            for half in (0, 1):
                arrived(half, 6, u - 2)
                arrived(half, 7, u - 2)
                start(half, 11, u - 2)

        @pl.when(u >= 3)
        def _():
            for half in (0, 1):
                for kind in (8, 9, 10, 11):
                    arrived(half, kind, u - 3)

        @pl.when((u >= 3) & (u < EARLY + 3))
        def _():
            def one(k, carry):
                late = (u == 4) & (k == 0)
                tile(jnp.where(late, ROW_CHUNKS - 1, k - (u == 4).astype(jnp.int32)), jnp.where(late, 0, u - 3))
                return carry

            lax.fori_loop(0, jnp.where(u == 3, ROW_CHUNKS - 1, jnp.where(u == 4, ROW_CHUNKS + 1, ROW_CHUNKS)), one, 0)

        return carry

    lax.fori_loop(0, PAIRS + 3, turn, 0)

    def settle(p, carry):
        for half in (0, 1):
            for kind in range(12):
                sent(half, kind, p)
        return carry

    lax.fori_loop(0, PAIRS, settle, 0)

    def left_settle(q, carry):
        for kind in range(4):
            left_sent(kind, q)
        return carry

    lax.fori_loop(0, ROW_CHUNKS, left_settle, 0)


def finish_kernel(a_ref, b_ref, part_ref, out_ref, last, sems):
    tiles, rows, width = last.shape
    done = pltpu.make_async_copy(part_ref, out_ref.at[:, : part_ref.shape[1]], sems.at[tiles])
    done.start()

    def out_copy(n):
        here = pl.ds(pl.multiple_of(n % ROW_CHUNKS * rows, rows), rows)
        cols = pl.ds(pl.multiple_of((n // ROW_CHUNKS + EARLY) * width, width), width)
        return pltpu.make_async_copy(last.at[n], out_ref.at[here, cols], sems.at[n])

    def one(n, carry):
        last[n] = tile_product(a_ref, b_ref, n % ROW_CHUNKS, n // ROW_CHUNKS + EARLY, width)
        out_copy(n).start()
        return carry

    def settle(n, carry):
        out_copy(n).wait()
        return carry

    lax.fori_loop(0, tiles, one, 0)
    lax.fori_loop(0, tiles, settle, 0)
    done.wait()


def per_device(left_block, right_block, slice_ids, mode_order):
    slices, rows_all, part_k = left_block.shape
    shard_k, values, columns = right_block.shape
    rows, width = rows_all // ROW_CHUNKS, columns // PAIRS
    bond = 4 * part_k
    late = (PAIRS - EARLY) * ROW_CHUNKS
    right = jnp.transpose(right_block, (1, 0, 2))
    vmem = pl.BlockSpec(memory_space=pltpu.VMEM)
    hbm = pl.BlockSpec(memory_space=pltpu.HBM)
    a, b, part = pl.pallas_call(
        gather_kernel,
        out_shape=(
            pltpu.VMEM((ROW_CHUNKS, 2 * rows, values * bond), jnp.bfloat16),
            pltpu.VMEM((values, 2, 4, 4, shard_k, columns), jnp.bfloat16),
            pltpu.VMEM((rows_all, EARLY * width), jnp.float32),
        ),
        in_specs=[hbm, hbm, hbm, vmem],
        out_specs=(vmem, vmem, vmem),
        scratch_shapes=[
            pltpu.SMEM(slice_ids.shape, jnp.int32),
            pltpu.SMEM(mode_order.shape, jnp.int32),
            pltpu.VMEM(left_block.shape, left_block.dtype),
            pltpu.VMEM((ROW_CHUNKS, 4, values, rows + 16, part_k), jnp.int16),
            pltpu.VMEM((bond, bond), jnp.bfloat16),
            pltpu.SemaphoreType.DMA((3,)),
            pltpu.SemaphoreType.DMA((24, PAIRS)),
            pltpu.SemaphoreType.DMA((24, PAIRS)),
            pltpu.SemaphoreType.DMA((4, ROW_CHUNKS)),
            pltpu.SemaphoreType.DMA((4, ROW_CHUNKS)),
        ],
        compiler_params=pltpu.CompilerParams(
            collective_id=0, has_side_effects=True, vmem_limit_bytes=20 << 20
        ),
    )(*(pltpu.with_memory_space_constraint(x, pltpu.HBM) for x in (slice_ids, mode_order, left_block)), right)
    return pl.pallas_call(
        finish_kernel,
        out_shape=jax.ShapeDtypeStruct((rows_all, columns), jnp.float32),
        in_specs=[vmem, vmem, vmem],
        out_specs=pl.BlockSpec(memory_space=pl.ANY),
        scratch_shapes=[
            pltpu.VMEM((late, rows, width), jnp.float32),
            pltpu.SemaphoreType.DMA((late + 1,)),
        ],
        compiler_params=pltpu.CompilerParams(vmem_limit_bytes=20 << 20),
    )(a, b, part)


def solution(mesh):
    in_specs = (P(None, ("row", "depth"), "col"), P(("row", "depth"), None, "col"), P(), P())
    out_specs = P(("row", "depth"), "col")
    return jax.shard_map(
        per_device, mesh=mesh, in_specs=in_specs, out_specs=out_specs, check_vma=False
    )
```

```python
import functools
import math

import jax
import jax.numpy as jnp
from jax import lax
from jax.experimental import pallas as pl
from jax.experimental.pallas import tpu as pltpu
from jax.sharding import PartitionSpec as P

MESH = pl.DeviceIdType.MESH
ROW_CHUNKS = 4
PAIRS = 4
EARLY = 3
CODE_TOP = 32000.0
STEPS_PER_OCTAVE = 16.0
LN2 = math.log(2.0)


def tile_product(a_ref, b_ref, i, j, width):
    cols = pl.ds(pl.multiple_of(j * width, width), width)
    b = b_ref[:, :, :, :, :, cols]
    b = b.reshape(-1, width)
    both = jnp.dot(a_ref[i], b, preferred_element_type=jnp.float32)
    rows = both.shape[0] // 2
    return both[:rows] + both[rows:]


def gather_kernel(
    ids_hbm,
    order_hbm,
    left_hbm,
    right_ref,
    a_ref,
    b_ref,
    part_ref,
    ids,
    order,
    left,
    code,
    pick,
    local,
    send,
    recv,
    left_send,
    left_recv,
):
    slices, rows_all, part_k = left.shape
    values, shard_k, columns = right_ref.shape
    rows, width = rows_all // ROW_CHUNKS, columns // PAIRS
    strip = width // 2
    bond = 4 * part_k

    row, c, y_lo = lax.axis_index("row"), lax.axis_index("col"), lax.axis_index("depth")
    core = row % 2
    y = (row // 2) % 2 * 2 + y_lo
    z = row // 4

    def place(y_at, z_at, core_at):
        return ((z_at * 2 + y_at // 2) * 2 + core_at, c, y_at % 2)

    def along_y(d):
        return place((y + d) % 4, z, core)

    def along_z(d):
        return place(y, (z + d) % 4, core)

    def along_x(d):
        return (row, (c + d) % 4, y_lo)

    sibling = place(y, z, 1 - core)

    barrier = pltpu.get_barrier_semaphore()
    for other in (along_y(1), along_y(3), along_z(1), along_z(3), along_x(1), along_x(3), sibling):
        pl.semaphore_signal(barrier, inc=1, device_id=other, device_id_type=MESH)

    staged = [
        pltpu.make_async_copy(left_hbm, left, local.at[0]),
        pltpu.make_async_copy(ids_hbm, ids, local.at[1]),
        pltpu.make_async_copy(order_hbm, order, local.at[2]),
    ]
    for one in staged:
        one.start()
    b_ref[:, core, z, y] = right_ref[...]

    def copy(ref, sems, at, device):
        return pltpu.make_async_remote_copy(
            src_ref=ref,
            dst_ref=ref,
            send_sem=sems[0].at[at],
            recv_sem=sems[1].at[at],
            device_id=device,
            device_id_type=MESH,
        )

    many, lefts = (send, recv), (left_send, left_recv)

    def moved(half, kind, p):
        cols = pl.ds(pl.multiple_of(p * width + half * strip, strip), strip)
        first, second = (along_y, along_z) if half == 0 else (along_z, along_y)
        at1, at2 = (y, z) if half == 0 else (z, y)

        def one(v, d):
            at = (at1 + d) % 4
            where = (z, at) if half == 0 else (at, y)
            return b_ref.at[(v, core, *where, slice(None), cols)]

        def group(v, plane, d):
            at = (at2 + d) % 4
            where = (at, slice(None)) if half == 0 else (slice(None), at)
            return b_ref.at[(v, plane, *where, slice(None), cols)]

        both = slice(None)
        if kind == 0:
            return one(both, 0), first(1), one(both, 3)
        if kind == 1:
            return one(both, 0), first(3), one(both, 1)
        if kind == 2:
            return one(0, 3), first(1), one(0, 2)
        if kind == 3:
            return one(1, 1), first(3), one(1, 2)
        if kind == 4:
            return group(both, core, 0), second(1), group(both, core, 3)
        if kind == 5:
            return group(both, core, 0), second(3), group(both, core, 1)
        if kind == 6:
            return group(0, core, 3), second(1), group(0, core, 2)
        if kind == 7:
            return group(1, core, 1), second(3), group(1, core, 2)
        d = (0, 3, 1, 2)[kind - 8]
        return group(both, core, d), sibling, group(both, 1 - core, d)

    def start(half, kind, p):
        ref, device, _ = moved(half, kind, p)
        copy(ref, many, (12 * half + kind, p), device).start()

    def arrived(half, kind, p):
        copy(moved(half, kind, p)[2], many, (12 * half + kind, p), sibling).wait_recv()

    def sent(half, kind, p):
        ref, device, _ = moved(half, kind, p)
        copy(ref, many, (12 * half + kind, p), device).wait_send()

    def left_moved(kind, q):
        before, after, far = (c + 3) % 4, (c + 1) % 4, (c + 2) % 4
        if kind == 0:
            return code.at[q, c], along_x(1), code.at[q, before]
        if kind == 1:
            return code.at[q, c], along_x(3), code.at[q, after]
        if kind == 2:
            return code.at[q, before, 0], along_x(1), code.at[q, far, 0]
        return code.at[q, after, 1], along_x(3), code.at[q, far, 1]

    def left_start(kind, q):
        ref, device, _ = left_moved(kind, q)
        copy(ref, lefts, (kind, q), device).start()

    def left_arrived(kind, q):
        copy(left_moved(kind, q)[2], lefts, (kind, q), sibling).wait_recv()

    def left_sent(kind, q):
        ref, device, _ = left_moved(kind, q)
        copy(ref, lefts, (kind, q), device).wait_send()

    def own_start(p):
        for half in (0, 1):
            start(half, 0, p)
            start(half, 1, p)

    def own_forward(p):
        for half in (0, 1):
            arrived(half, 0, p)
            start(half, 2, p)
            arrived(half, 1, p)
            start(half, 3, p)

    pl.semaphore_wait(barrier, 7)
    for p in range(PAIRS):
        own_start(p)
    for one in staged:
        one.wait()

    weights = [
        [jnp.where(ids[s] == v, 1.0, 0.0).astype(jnp.float32) for s in range(slices)]
        for v in range(values)
    ]

    def encode(q, carry):
        here = pl.ds(pl.multiple_of(q * rows, rows), rows)
        blocks = [left[s, here, :].astype(jnp.float32) for s in range(slices)]
        for v in range(values):
            total = blocks[0] * weights[v][0]
            for s in range(1, slices):
                total = total + blocks[s] * weights[v][s]
            top = jnp.max(jnp.abs(total), axis=0, keepdims=True)
            top = jnp.maximum(top, 2.0**-110)
            level = jnp.ceil(jnp.log(top) * (STEPS_PER_OCTAVE / LN2))
            scale = jnp.exp(level * (-LN2 / STEPS_PER_OCTAVE)) * CODE_TOP
            code[q, c, v, :rows, :] = jnp.round(total * scale).astype(jnp.int32).astype(jnp.int16)
            code[q, c, v, rows:, :] = jnp.broadcast_to(level, (16, part_k)).astype(jnp.int32).astype(jnp.int16)

        @pl.when(q < 2)
        def _():
            left_start(0, q)
            left_start(1, q)

        return carry

    lax.fori_loop(0, 2, encode, 0)
    for p in range(PAIRS):
        own_forward(p)
    lax.fori_loop(2, ROW_CHUNKS, encode, 0)

    place_at = lax.broadcasted_iota(jnp.int32, (8, bond), 1)
    j = place_at & 15
    at_y, at_z, plane = (place_at >> 4) & 3, (place_at >> 6) & 3, place_at >> 8
    shard = at_z * 8 + (at_y >> 1) * 4 + plane * 2 + (at_y & 1)
    logical = shard * shard_k + j
    stored = jnp.zeros((8, bond), jnp.int32)
    for bit in range(order.shape[0]):
        stored = stored + ((logical >> bit) & 1) * jnp.left_shift(jnp.int32(1), order[bit])
    hit = lax.broadcasted_iota(jnp.int32, (bond, bond), 0) == stored[:1]
    pick[...] = jnp.where(hit, 1.0, 0.0).astype(jnp.bfloat16)

    def decode(q):
        parts = []
        for v in range(values):
            high, low = [], []
            for at in range(4):
                level = code[q, at, v, rows:, :].astype(jnp.int32).astype(jnp.float32)[:1]
                scale = jnp.exp(level * (LN2 / STEPS_PER_OCTAVE)) * (1.0 / CODE_TOP)
                x = code[q, at, v, :rows, :].astype(jnp.int32).astype(jnp.float32) * scale
                h = x.astype(jnp.bfloat16)
                high.append(h)
                low.append((x - h.astype(jnp.float32)).astype(jnp.bfloat16))
            parts += [jnp.concatenate(high, axis=1), jnp.concatenate(low, axis=1)]
        picked = jnp.dot(
            jnp.concatenate(parts, axis=0), pick[...], preferred_element_type=jnp.float32
        ).astype(jnp.bfloat16)
        for v in range(values):
            a_ref[q, :, v * bond : (v + 1) * bond] = picked[2 * rows * v : 2 * rows * (v + 1)]

    def tile(q, p):
        here = pl.ds(pl.multiple_of(q * rows, rows), rows)
        cols = pl.ds(pl.multiple_of(p * width, width), width)
        part_ref[here, cols] = tile_product(a_ref, b_ref, q, p, width)

    def tiles(q_from, q_to, p_from, p_to):
        many_q = q_to - q_from

        def one(n, carry):
            tile(q_from + n % many_q, p_from + n // many_q)
            return carry

        lax.fori_loop(0, many_q * (p_to - p_from), one, 0)

    def group_start(p):
        for half in (0, 1):
            arrived(half, 2, p)
            arrived(half, 3, p)
            start(half, 4, p)
            start(half, 5, p)
            start(half, 8, p)

    def group_forward(p):
        for half in (0, 1):
            arrived(half, 4, p)
            start(half, 6, p)
            start(half, 9, p)
            arrived(half, 5, p)
            start(half, 7, p)
            start(half, 10, p)

    def group_last(p):
        for half in (0, 1):
            arrived(half, 6, p)
            arrived(half, 7, p)
            start(half, 11, p)

    def whole(p):
        for half in (0, 1):
            for kind in (8, 9, 10, 11):
                arrived(half, kind, p)

    def left_forward(q):
        left_arrived(0, q)
        left_start(2, q)
        left_arrived(1, q)
        left_start(3, q)
        if q + 2 < ROW_CHUNKS:
            left_start(0, q + 2)
            left_start(1, q + 2)

    def left_whole(q):
        left_arrived(2, q)
        left_arrived(3, q)
        decode(q)

    group_start(0)
    group_start(1)
    left_forward(0)
    group_forward(0)
    group_start(2)
    left_forward(1)
    left_whole(0)
    group_forward(1)
    group_start(3)
    left_forward(2)
    group_last(0)
    whole(0)
    tiles(0, 1, 0, 1)
    left_whole(1)
    left_forward(3)
    tiles(1, 2, 0, 1)
    group_forward(2)
    group_last(1)
    whole(1)
    tiles(0, 2, 1, 2)
    group_forward(3)
    group_last(2)
    left_whole(2)
    tiles(2, 3, 0, 2)
    whole(2)
    group_last(3)
    tiles(0, 3, 2, 3)
    left_whole(3)
    tiles(3, 4, 0, 3)
    whole(3)

    def settle(p, carry):
        for half in (0, 1):
            for kind in range(12):
                sent(half, kind, p)
        return carry

    lax.fori_loop(0, PAIRS, settle, 0)

    def left_settle(q, carry):
        for kind in range(4):
            left_sent(kind, q)
        return carry

    lax.fori_loop(0, ROW_CHUNKS, left_settle, 0)


def finish_kernel(a_ref, b_ref, part_ref, out_ref, last, sems):
    tiles, rows, width = last.shape
    done = pltpu.make_async_copy(part_ref, out_ref.at[:, : part_ref.shape[1]], sems.at[tiles])
    done.start()

    def out_copy(n):
        here = pl.ds(pl.multiple_of(n % ROW_CHUNKS * rows, rows), rows)
        cols = pl.ds(pl.multiple_of((n // ROW_CHUNKS + EARLY) * width, width), width)
        return pltpu.make_async_copy(last.at[n], out_ref.at[here, cols], sems.at[n])

    def one(n, carry):
        last[n] = tile_product(a_ref, b_ref, n % ROW_CHUNKS, n // ROW_CHUNKS + EARLY, width)
        out_copy(n).start()
        return carry

    def settle(n, carry):
        out_copy(n).wait()
        return carry

    lax.fori_loop(0, tiles, one, 0)
    lax.fori_loop(0, tiles, settle, 0)
    done.wait()


def per_device(left_block, right_block, slice_ids, mode_order):
    slices, rows_all, part_k = left_block.shape
    shard_k, values, columns = right_block.shape
    rows, width = rows_all // ROW_CHUNKS, columns // PAIRS
    bond = 4 * part_k
    late = (PAIRS - EARLY) * ROW_CHUNKS
    right = jnp.transpose(right_block, (1, 0, 2))
    vmem = pl.BlockSpec(memory_space=pltpu.VMEM)
    hbm = pl.BlockSpec(memory_space=pltpu.HBM)
    a, b, part = pl.pallas_call(
        gather_kernel,
        out_shape=(
            pltpu.VMEM((ROW_CHUNKS, 2 * rows, values * bond), jnp.bfloat16),
            pltpu.VMEM((values, 2, 4, 4, shard_k, columns), jnp.bfloat16),
            pltpu.VMEM((rows_all, EARLY * width), jnp.float32),
        ),
        in_specs=[hbm, hbm, hbm, vmem],
        out_specs=(vmem, vmem, vmem),
        scratch_shapes=[
            pltpu.SMEM(slice_ids.shape, jnp.int32),
            pltpu.SMEM(mode_order.shape, jnp.int32),
            pltpu.VMEM(left_block.shape, left_block.dtype),
            pltpu.VMEM((ROW_CHUNKS, 4, values, rows + 16, part_k), jnp.int16),
            pltpu.VMEM((bond, bond), jnp.bfloat16),
            pltpu.SemaphoreType.DMA((3,)),
            pltpu.SemaphoreType.DMA((24, PAIRS)),
            pltpu.SemaphoreType.DMA((24, PAIRS)),
            pltpu.SemaphoreType.DMA((4, ROW_CHUNKS)),
            pltpu.SemaphoreType.DMA((4, ROW_CHUNKS)),
        ],
        compiler_params=pltpu.CompilerParams(
            collective_id=0, has_side_effects=True, vmem_limit_bytes=20 << 20
        ),
    )(*(pltpu.with_memory_space_constraint(x, pltpu.HBM) for x in (slice_ids, mode_order, left_block)), right)
    return pl.pallas_call(
        finish_kernel,
        out_shape=jax.ShapeDtypeStruct((rows_all, columns), jnp.float32),
        in_specs=[vmem, vmem, vmem],
        out_specs=pl.BlockSpec(memory_space=pl.ANY),
        scratch_shapes=[
            pltpu.VMEM((late, rows, width), jnp.float32),
            pltpu.SemaphoreType.DMA((late + 1,)),
        ],
        compiler_params=pltpu.CompilerParams(vmem_limit_bytes=20 << 20),
    )(a, b, part)


def solution(mesh):
    in_specs = (P(None, ("row", "depth"), "col"), P(("row", "depth"), None, "col"), P(), P())
    out_specs = P(("row", "depth"), "col")
    return jax.shard_map(
        per_device, mesh=mesh, in_specs=in_specs, out_specs=out_specs, check_vma=False
    )
```

```python
import functools
import math

import jax
import jax.numpy as jnp
from jax import lax
from jax.experimental import pallas as pl
from jax.experimental.pallas import tpu as pltpu
from jax.sharding import PartitionSpec as P

MESH = pl.DeviceIdType.MESH
ROW_CHUNKS = 4
PAIRS = 4
AHEAD = 2
EARLY = 3
CODE_TOP = 32000.0
STEPS_PER_OCTAVE = 16.0
LN2 = math.log(2.0)


def tile_product(a_ref, b_ref, q, p):
    halves = [b_ref[p, half] for half in (0, 1)]
    strip = halves[0].shape[-1]
    b = jnp.concatenate([half.reshape(-1, strip) for half in halves], axis=1)
    both = jnp.dot(a_ref[q], b, preferred_element_type=jnp.float32)
    rows = both.shape[0] // 2
    return both[:rows] + both[rows:]


def gather_kernel(
    ids_hbm,
    order_hbm,
    left_hbm,
    right_ref,
    a_ref,
    b_ref,
    part_ref,
    ids,
    order,
    left,
    code,
    pick,
    local,
    send,
    recv,
    left_recv,
):
    slices, rows_all, part_k = left.shape
    values, shard_k, columns = right_ref.shape
    rows, width = rows_all // ROW_CHUNKS, columns // PAIRS
    strip = width // 2
    bond = 4 * part_k

    row, c, y_lo = lax.axis_index("row"), lax.axis_index("col"), lax.axis_index("depth")
    core = row % 2
    y = (row // 2) % 2 * 2 + y_lo
    z = row // 4

    def place(y_at, z_at, core_at):
        return ((z_at * 2 + y_at // 2) * 2 + core_at, c, y_at % 2)

    def along_y(d):
        return place((y + d) % 4, z, core)

    def along_z(d):
        return place(y, (z + d) % 4, core)

    def along_x(d):
        return (row, (c + d) % 4, y_lo)

    sibling = place(y, z, 1 - core)

    barrier = pltpu.get_barrier_semaphore()
    for other in (along_y(1), along_y(3), along_z(1), along_z(3), along_x(1), along_x(3), sibling):
        pl.semaphore_signal(barrier, inc=1, device_id=other, device_id_type=MESH)

    staged = [
        pltpu.make_async_copy(left_hbm, left, local.at[0]),
        pltpu.make_async_copy(ids_hbm, ids, local.at[1]),
        pltpu.make_async_copy(order_hbm, order, local.at[2]),
    ]
    for one in staged:
        one.start()
    for p in range(PAIRS):
        for half in (0, 1):
            at = p * width + half * strip
            b_ref[p, half, :, core, z, y] = right_ref[:, :, at : at + strip]

    def copy(ref, signals, device):
        return pltpu.make_async_remote_copy(
            src_ref=ref,
            dst_ref=ref,
            send_sem=signals[0],
            recv_sem=signals[1],
            device_id=device,
            device_id_type=MESH,
        )

    def moved(half, kind, p):
        first, second = (along_y, along_z) if half == 0 else (along_z, along_y)
        at1, at2 = (y, z) if half == 0 else (z, y)
        both = slice(None)

        def one(v, d):
            at = (at1 + d) % 4
            where = (z, at) if half == 0 else (at, y)
            return b_ref.at[(pl.ds(p * AHEAD, AHEAD), half, v, core, *where)]

        def group(v, d):
            at = (at2 + d) % 4
            where = (at, both) if half == 0 else (both, at)
            return b_ref.at[(p, half, v, core, *where)]

        if kind == 0:
            return one(both, 0), first(1), one(both, 3)
        if kind == 1:
            return one(both, 0), first(3), one(both, 1)
        if kind == 2:
            return one(0, 3), first(1), one(0, 2)
        if kind == 3:
            return one(1, 1), first(3), one(1, 2)
        if kind == 4:
            return group(both, 0), second(1), group(both, 3)
        if kind == 5:
            return group(both, 0), second(3), group(both, 1)
        if kind == 6:
            return group(0, 3), second(1), group(0, 2)
        if kind == 7:
            return group(1, 1), second(3), group(1, 2)
        return b_ref.at[p, :, :, core], sibling, b_ref.at[p, :, :, 1 - core]

    def sems(half, kind, p):
        return send.at[kind // 2], recv.at[half, kind, p]

    def start(half, kind, p):
        ref, device, _ = moved(half, kind, p)
        copy(ref, sems(half, kind, p), device).start()

    def arrived(half, kind, p):
        copy(moved(half, kind, p)[2], sems(half, kind, p), sibling).wait_recv()

    def left_moved(kind, q):
        before, after, far = (c + 3) % 4, (c + 1) % 4, (c + 2) % 4
        if kind == 0:
            return code.at[q, c], along_x(1), code.at[q, before]
        if kind == 1:
            return code.at[q, c], along_x(3), code.at[q, after]
        if kind == 2:
            return code.at[q, before, 0], along_x(1), code.at[q, far, 0]
        return code.at[q, after, 1], along_x(3), code.at[q, far, 1]

    def left_sems(kind, q):
        return send.at[5 + kind // 2], left_recv.at[kind, q]

    def left_start(kind, q):
        ref, device, _ = left_moved(kind, q)
        copy(ref, left_sems(kind, q), device).start()

    def left_arrived(kind, q):
        copy(left_moved(kind, q)[2], left_sems(kind, q), sibling).wait_recv()

    def own_start(p):
        for half in (0, 1):
            start(half, 0, p)
            start(half, 1, p)

    def own_forward(p):
        for half in (0, 1):
            arrived(half, 0, p)
            start(half, 2, p)
            arrived(half, 1, p)
            start(half, 3, p)

    pl.semaphore_wait(barrier, 7)
    for p in range(PAIRS // AHEAD):
        own_start(p)
    for one in staged:
        one.wait()

    weights = [
        [jnp.where(ids[s] == v, 1.0, 0.0).astype(jnp.float32) for s in range(slices)]
        for v in range(values)
    ]

    def encode(q, carry):
        here = pl.ds(pl.multiple_of(q * rows, rows), rows)
        blocks = [left[s, here, :].astype(jnp.float32) for s in range(slices)]
        for v in range(values):
            total = blocks[0] * weights[v][0]
            for s in range(1, slices):
                total = total + blocks[s] * weights[v][s]
            top = jnp.max(jnp.abs(total), axis=0, keepdims=True)
            top = jnp.maximum(top, 2.0**-110)
            level = jnp.ceil(jnp.log(top) * (STEPS_PER_OCTAVE / LN2))
            scale = jnp.exp(level * (-LN2 / STEPS_PER_OCTAVE)) * CODE_TOP
            code[q, c, v, :rows, :] = jnp.round(total * scale).astype(jnp.int32).astype(jnp.int16)
            code[q, c, v, rows:, :] = jnp.broadcast_to(level, (16, part_k)).astype(jnp.int32).astype(jnp.int16)

        @pl.when(q < 2)
        def _():
            left_start(0, q)
            left_start(1, q)

        return carry

    lax.fori_loop(0, 2, encode, 0)
    for p in range(PAIRS // AHEAD):
        own_forward(p)
    lax.fori_loop(2, ROW_CHUNKS, encode, 0)

    place_at = lax.broadcasted_iota(jnp.int32, (8, bond), 1)
    j = place_at & 15
    at_y, at_z, plane = (place_at >> 4) & 3, (place_at >> 6) & 3, place_at >> 8
    shard = at_z * 8 + (at_y >> 1) * 4 + plane * 2 + (at_y & 1)
    logical = shard * shard_k + j
    stored = jnp.zeros((8, bond), jnp.int32)
    for bit in range(order.shape[0]):
        stored = stored + ((logical >> bit) & 1) * jnp.left_shift(jnp.int32(1), order[bit])
    hit = lax.broadcasted_iota(jnp.int32, (bond, bond), 0) == stored[:1]
    pick[...] = jnp.where(hit, 1.0, 0.0).astype(jnp.bfloat16)

    def decode(q):
        parts = []
        for v in range(values):
            high, low = [], []
            for at in range(4):
                level = code[q, at, v, rows:, :].astype(jnp.int32).astype(jnp.float32)[:1]
                scale = jnp.exp(level * (LN2 / STEPS_PER_OCTAVE)) * (1.0 / CODE_TOP)
                x = code[q, at, v, :rows, :].astype(jnp.int32).astype(jnp.float32) * scale
                h = x.astype(jnp.bfloat16)
                high.append(h)
                low.append((x - h.astype(jnp.float32)).astype(jnp.bfloat16))
            parts += [jnp.concatenate(high, axis=1), jnp.concatenate(low, axis=1)]
        picked = jnp.dot(
            jnp.concatenate(parts, axis=0), pick[...], preferred_element_type=jnp.float32
        ).astype(jnp.bfloat16)
        for v in range(values):
            a_ref[q, :, v * bond : (v + 1) * bond] = picked[2 * rows * v : 2 * rows * (v + 1)]

    def tile(q, p):
        here = pl.ds(pl.multiple_of(q * rows, rows), rows)
        cols = pl.ds(pl.multiple_of(p * width, width), width)
        part_ref[here, cols] = tile_product(a_ref, b_ref, q, p)

    def tiles(q_from, q_to, p_from, p_to):
        many_q = q_to - q_from

        def one(n, carry):
            tile(q_from + n % many_q, p_from + n // many_q)
            return carry

        lax.fori_loop(0, many_q * (p_to - p_from), one, 0)

    def group_start(p):
        for half in (0, 1):
            if p % AHEAD == 0:
                arrived(half, 2, p // AHEAD)
                arrived(half, 3, p // AHEAD)
            start(half, 4, p)
            start(half, 5, p)

    def group_forward(p):
        for half in (0, 1):
            arrived(half, 4, p)
            start(half, 6, p)
            arrived(half, 5, p)
            start(half, 7, p)

    def group_last(p):
        for half in (0, 1):
            arrived(half, 6, p)
            arrived(half, 7, p)
        start(0, 8, p)

    def whole(p):
        arrived(0, 8, p)

    def left_forward(q):
        left_arrived(0, q)
        left_start(2, q)
        left_arrived(1, q)
        left_start(3, q)
        if q + 2 < ROW_CHUNKS:
            left_start(0, q + 2)
            left_start(1, q + 2)

    def left_whole(q):
        left_arrived(2, q)
        left_arrived(3, q)
        decode(q)

    group_start(0)
    group_start(1)
    left_forward(0)
    group_forward(0)
    group_start(2)
    left_forward(1)
    left_whole(0)
    group_forward(1)
    group_start(3)
    left_forward(2)
    group_last(0)
    whole(0)
    tiles(0, 1, 0, 1)
    left_whole(1)
    left_forward(3)
    tiles(1, 2, 0, 1)
    group_forward(2)
    group_last(1)
    whole(1)
    tiles(0, 2, 1, 2)
    group_forward(3)
    group_last(2)
    left_whole(2)
    tiles(2, 3, 0, 2)
    whole(2)
    group_last(3)
    tiles(0, 3, 2, 3)
    left_whole(3)
    tiles(3, 4, 0, 3)
    whole(3)

    sizes = (
        b_ref.at[0, 0, 0],
        b_ref.at[0, 0, 0, 0],
        b_ref.at[0],
        b_ref.at[0, 0],
        b_ref.at[pl.ds(0, PAIRS // 2)],
        code.at[pl.ds(0, 2)],
        code.at[0],
    )
    for n, size in enumerate(sizes):
        copy(size, (send.at[n], recv.at[0, 0, 0]), sibling).wait_send()


def finish_kernel(a_ref, b_ref, part_ref, out_ref, last, sems):
    tiles, rows, width = last.shape
    done = pltpu.make_async_copy(part_ref, out_ref.at[:, : part_ref.shape[1]], sems.at[tiles])
    done.start()

    def out_copy(n):
        here = pl.ds(pl.multiple_of(n % ROW_CHUNKS * rows, rows), rows)
        cols = pl.ds(pl.multiple_of((n // ROW_CHUNKS + EARLY) * width, width), width)
        return pltpu.make_async_copy(last.at[n], out_ref.at[here, cols], sems.at[n])

    def one(n, carry):
        last[n] = tile_product(a_ref, b_ref, n % ROW_CHUNKS, n // ROW_CHUNKS + EARLY)
        out_copy(n).start()
        return carry

    def settle(n, carry):
        out_copy(n).wait()
        return carry

    lax.fori_loop(0, tiles, one, 0)
    lax.fori_loop(0, tiles, settle, 0)
    done.wait()


def per_device(left_block, right_block, slice_ids, mode_order):
    slices, rows_all, part_k = left_block.shape
    shard_k, values, columns = right_block.shape
    rows, width = rows_all // ROW_CHUNKS, columns // PAIRS
    bond = 4 * part_k
    late = (PAIRS - EARLY) * ROW_CHUNKS
    right = jnp.transpose(right_block, (1, 0, 2))
    vmem = pl.BlockSpec(memory_space=pltpu.VMEM)
    hbm = pl.BlockSpec(memory_space=pltpu.HBM)
    a, b, part = pl.pallas_call(
        gather_kernel,
        out_shape=(
            pltpu.VMEM((ROW_CHUNKS, 2 * rows, values * bond), jnp.bfloat16),
            pltpu.VMEM((PAIRS, 2, values, 2, 4, 4, shard_k, width // 2), jnp.bfloat16),
            pltpu.VMEM((rows_all, EARLY * width), jnp.float32),
        ),
        in_specs=[hbm, hbm, hbm, vmem],
        out_specs=(vmem, vmem, vmem),
        scratch_shapes=[
            pltpu.SMEM(slice_ids.shape, jnp.int32),
            pltpu.SMEM(mode_order.shape, jnp.int32),
            pltpu.VMEM(left_block.shape, left_block.dtype),
            pltpu.VMEM((ROW_CHUNKS, 4, values, rows + 16, part_k), jnp.int16),
            pltpu.VMEM((bond, bond), jnp.bfloat16),
            pltpu.SemaphoreType.DMA((3,)),
            pltpu.SemaphoreType.DMA((7,)),
            pltpu.SemaphoreType.DMA((2, 9, PAIRS)),
            pltpu.SemaphoreType.DMA((4, ROW_CHUNKS)),
        ],
        compiler_params=pltpu.CompilerParams(
            collective_id=0, has_side_effects=True, vmem_limit_bytes=20 << 20
        ),
    )(*(pltpu.with_memory_space_constraint(x, pltpu.HBM) for x in (slice_ids, mode_order, left_block)), right)
    return pl.pallas_call(
        finish_kernel,
        out_shape=jax.ShapeDtypeStruct((rows_all, columns), jnp.float32),
        in_specs=[vmem, vmem, vmem],
        out_specs=pl.BlockSpec(memory_space=pl.ANY),
        scratch_shapes=[
            pltpu.VMEM((late, rows, width), jnp.float32),
            pltpu.SemaphoreType.DMA((late + 1,)),
        ],
        compiler_params=pltpu.CompilerParams(vmem_limit_bytes=20 << 20),
    )(a, b, part)


def solution(mesh):
    in_specs = (P(None, ("row", "depth"), "col"), P(("row", "depth"), None, "col"), P(), P())
    out_specs = P(("row", "depth"), "col")
    return jax.shard_map(
        per_device, mesh=mesh, in_specs=in_specs, out_specs=out_specs, check_vma=False
    )
```

```python
import functools
import math

import jax
import jax.numpy as jnp
from jax import lax
from jax.experimental import pallas as pl
from jax.experimental.pallas import tpu as pltpu
from jax.sharding import PartitionSpec as P

MESH = pl.DeviceIdType.MESH
ROW_CHUNKS = 4
PAIRS = 8
AHEAD = 4
EARLY = 6
CODE_TOP = 32000.0
STEPS_PER_OCTAVE = 16.0
LN2 = math.log(2.0)


def tile_product(a_ref, b_ref, q, p):
    halves = [b_ref[p, half] for half in (0, 1)]
    strip = halves[0].shape[-1]
    b = jnp.concatenate([half.reshape(-1, strip) for half in halves], axis=1)
    a = a_ref[pl.ds(2 * q, 2)]
    rows = a.shape[1] // 2
    both = jnp.dot(a.reshape(-1, a.shape[2]), b, preferred_element_type=jnp.float32)
    both = both.reshape(2, 2, rows, both.shape[1])
    return (both[:, 0] + both[:, 1]).reshape(2 * rows, both.shape[3])


def gather_kernel(
    ids_hbm,
    order_hbm,
    left_hbm,
    right_ref,
    a_ref,
    b_ref,
    part_ref,
    ids,
    order,
    left,
    code,
    pick,
    local,
    send,
    recv,
    left_recv,
):
    slices, rows_all, part_k = left.shape
    values, shard_k, columns = right_ref.shape
    rows, width = rows_all // ROW_CHUNKS, columns // PAIRS
    strip = width // 2
    bond = 4 * part_k

    row, c, y_lo = lax.axis_index("row"), lax.axis_index("col"), lax.axis_index("depth")
    core = row % 2
    y = (row // 2) % 2 * 2 + y_lo
    z = row // 4

    def place(y_at, z_at, core_at):
        return ((z_at * 2 + y_at // 2) * 2 + core_at, c, y_at % 2)

    def along_y(d):
        return place((y + d) % 4, z, core)

    def along_z(d):
        return place(y, (z + d) % 4, core)

    def along_x(d):
        return (row, (c + d) % 4, y_lo)

    sibling = place(y, z, 1 - core)

    barrier = pltpu.get_barrier_semaphore()
    for other in (along_y(1), along_y(3), along_z(1), along_z(3), along_x(1), along_x(3), sibling):
        pl.semaphore_signal(barrier, inc=1, device_id=other, device_id_type=MESH)

    staged = [
        pltpu.make_async_copy(left_hbm, left, local.at[0]),
        pltpu.make_async_copy(ids_hbm, ids, local.at[1]),
        pltpu.make_async_copy(order_hbm, order, local.at[2]),
    ]
    for one in staged:
        one.start()
    for p in range(PAIRS):
        for half in (0, 1):
            at = p * width + half * strip
            b_ref[p, half, :, core, z, y] = right_ref[:, :, at : at + strip]

    def copy(ref, signals, device):
        return pltpu.make_async_remote_copy(
            src_ref=ref,
            dst_ref=ref,
            send_sem=signals[0],
            recv_sem=signals[1],
            device_id=device,
            device_id_type=MESH,
        )

    def moved(half, kind, p):
        first, second = (along_y, along_z) if half == 0 else (along_z, along_y)
        at1, at2 = (y, z) if half == 0 else (z, y)
        both = slice(None)

        def one(v, d):
            at = (at1 + d) % 4
            where = (z, at) if half == 0 else (at, y)
            return b_ref.at[(pl.ds(p * AHEAD, AHEAD), half, v, core, *where)]

        def group(v, d):
            at = (at2 + d) % 4
            where = (at, both) if half == 0 else (both, at)
            return b_ref.at[(p, half, v, core, *where)]

        if kind == 0:
            return one(both, 0), first(1), one(both, 3)
        if kind == 1:
            return one(both, 0), first(3), one(both, 1)
        if kind == 2:
            return one(0, 3), first(1), one(0, 2)
        if kind == 3:
            return one(1, 1), first(3), one(1, 2)
        if kind == 4:
            return group(both, 0), second(1), group(both, 3)
        if kind == 5:
            return group(both, 0), second(3), group(both, 1)
        if kind == 6:
            return group(0, 3), second(1), group(0, 2)
        if kind == 7:
            return group(1, 1), second(3), group(1, 2)
        return b_ref.at[p, :, :, core], sibling, b_ref.at[p, :, :, 1 - core]

    def sems(half, kind, p):
        return send.at[kind // 2], recv.at[half, kind, p]

    def start(half, kind, p):
        ref, device, _ = moved(half, kind, p)
        copy(ref, sems(half, kind, p), device).start()

    def arrived(half, kind, p):
        copy(moved(half, kind, p)[2], sems(half, kind, p), sibling).wait_recv()

    def left_moved(kind, q):
        before, after, far = (c + 3) % 4, (c + 1) % 4, (c + 2) % 4
        if kind == 0:
            return code.at[q, c], along_x(1), code.at[q, before]
        if kind == 1:
            return code.at[q, c], along_x(3), code.at[q, after]
        if kind == 2:
            return code.at[q, before, 0], along_x(1), code.at[q, far, 0]
        return code.at[q, after, 1], along_x(3), code.at[q, far, 1]

    def left_sems(kind, q):
        return send.at[5 + kind // 2], left_recv.at[kind, q]

    def left_start(kind, q):
        ref, device, _ = left_moved(kind, q)
        copy(ref, left_sems(kind, q), device).start()

    def left_arrived(kind, q):
        copy(left_moved(kind, q)[2], left_sems(kind, q), sibling).wait_recv()

    def own_start(p):
        for half in (0, 1):
            start(half, 0, p)
            start(half, 1, p)

    def own_forward(p):
        for half in (0, 1):
            arrived(half, 0, p)
            start(half, 2, p)
            arrived(half, 1, p)
            start(half, 3, p)

    pl.semaphore_wait(barrier, 7)
    for p in range(PAIRS // AHEAD):
        own_start(p)
    for one in staged:
        one.wait()

    weights = [
        [jnp.where(ids[s] == v, 1.0, 0.0).astype(jnp.float32) for s in range(slices)]
        for v in range(values)
    ]

    def encode(q, carry):
        here = pl.ds(pl.multiple_of(q * rows, rows), rows)
        blocks = [left[s, here, :].astype(jnp.float32) for s in range(slices)]
        for v in range(values):
            total = blocks[0] * weights[v][0]
            for s in range(1, slices):
                total = total + blocks[s] * weights[v][s]
            top = jnp.max(jnp.abs(total), axis=0, keepdims=True)
            top = jnp.maximum(top, 2.0**-110)
            level = jnp.ceil(jnp.log(top) * (STEPS_PER_OCTAVE / LN2))
            scale = jnp.exp(level * (-LN2 / STEPS_PER_OCTAVE)) * CODE_TOP
            code[q, c, v, :rows, :] = jnp.round(total * scale).astype(jnp.int32).astype(jnp.int16)
            code[q, c, v, rows:, :] = jnp.broadcast_to(level, (16, part_k)).astype(jnp.int32).astype(jnp.int16)

        @pl.when(q < 2)
        def _():
            left_start(0, q)
            left_start(1, q)

        return carry

    lax.fori_loop(0, 2, encode, 0)
    for p in range(PAIRS // AHEAD):
        own_forward(p)
    lax.fori_loop(2, ROW_CHUNKS, encode, 0)

    place_at = lax.broadcasted_iota(jnp.int32, (8, bond), 1)
    j = place_at & 15
    at_y, at_z, plane = (place_at >> 4) & 3, (place_at >> 6) & 3, place_at >> 8
    shard = at_z * 8 + (at_y >> 1) * 4 + plane * 2 + (at_y & 1)
    logical = shard * shard_k + j
    stored = jnp.zeros((8, bond), jnp.int32)
    for bit in range(order.shape[0]):
        stored = stored + ((logical >> bit) & 1) * jnp.left_shift(jnp.int32(1), order[bit])
    hit = lax.broadcasted_iota(jnp.int32, (bond, bond), 0) == stored[:1]
    pick[...] = jnp.where(hit, 1.0, 0.0).astype(jnp.bfloat16)

    def decode(q):
        parts = []
        for v in range(values):
            high, low = [], []
            for at in range(4):
                level = code[q, at, v, rows:, :].astype(jnp.int32).astype(jnp.float32)[:1]
                scale = jnp.exp(level * (LN2 / STEPS_PER_OCTAVE)) * (1.0 / CODE_TOP)
                x = code[q, at, v, :rows, :].astype(jnp.int32).astype(jnp.float32) * scale
                h = x.astype(jnp.bfloat16)
                high.append(h)
                low.append((x - h.astype(jnp.float32)).astype(jnp.bfloat16))
            parts += [jnp.concatenate(high, axis=1), jnp.concatenate(low, axis=1)]
        picked = jnp.dot(
            jnp.concatenate(parts, axis=0), pick[...], preferred_element_type=jnp.float32
        ).astype(jnp.bfloat16)
        for v in range(values):
            a_ref[q, :, v * bond : (v + 1) * bond] = picked[2 * rows * v : 2 * rows * (v + 1)]

    def tile(q, p):
        part_ref[2 * q * rows : 2 * (q + 1) * rows, p * width : (p + 1) * width] = tile_product(a_ref, b_ref, q, p)

    def group_start(p):
        for half in (0, 1):
            if p % AHEAD == 0:
                arrived(half, 2, p // AHEAD)
                arrived(half, 3, p // AHEAD)
            start(half, 4, p)
            start(half, 5, p)

    def group_forward(p):
        for half in (0, 1):
            arrived(half, 4, p)
            start(half, 6, p)
            arrived(half, 5, p)
            start(half, 7, p)

    def group_last(p):
        for half in (0, 1):
            arrived(half, 6, p)
            arrived(half, 7, p)
        start(0, 8, p)

    def whole(p):
        arrived(0, 8, p)

    def left_forward(q):
        left_arrived(0, q)
        left_start(2, q)
        left_arrived(1, q)
        left_start(3, q)
        if q + 2 < ROW_CHUNKS:
            left_start(0, q + 2)
            left_start(1, q + 2)

    def left_whole(q):
        left_arrived(2, q)
        left_arrived(3, q)
        decode(q)

    group_start(0)
    group_start(1)
    left_forward(0)
    group_forward(0)
    group_start(2)
    left_forward(1)
    left_whole(0)
    for p in range(PAIRS):
        if p + 1 < PAIRS:
            group_forward(p + 1)
        if p + 3 < PAIRS:
            group_start(p + 3)
        group_last(p)
        if p == 0:
            left_forward(2)
            left_whole(1)
        if p == 1:
            left_forward(3)
        if p == 2:
            left_whole(2)
            left_whole(3)
            tile(1, 0)
        if p == 3:
            tile(1, 1)
        if 3 <= p <= EARLY:
            tile(1, p - 1)
        whole(p)
        if p < EARLY:
            tile(0, p)

    sizes = (
        b_ref.at[0, 0],
        b_ref.at[0, 0, 0],
        b_ref.at[pl.ds(0, PAIRS // 4)],
        b_ref.at[0],
        b_ref.at[pl.ds(0, PAIRS // 2)],
        code.at[pl.ds(0, 2)],
        code.at[0],
    )
    for n, size in enumerate(sizes):
        copy(size, (send.at[n], recv.at[0, 0, 0]), sibling).wait_send()


def finish_kernel(a_ref, b_ref, part_ref, out_ref, last, sems):
    tiles, rows, width = last.shape
    done = pltpu.make_async_copy(part_ref, out_ref.at[:, : part_ref.shape[1]], sems.at[tiles])
    done.start()

    def out_copy(n):
        here = pl.ds(pl.multiple_of(n % 2 * rows, rows), rows)
        cols = pl.ds(pl.multiple_of((n // 2 + EARLY) * width, width), width)
        return pltpu.make_async_copy(last.at[n], out_ref.at[here, cols], sems.at[n])

    def one(n, carry):
        last[n] = tile_product(a_ref, b_ref, n % 2, n // 2 + EARLY)
        out_copy(n).start()
        return carry

    def settle(n, carry):
        out_copy(n).wait()
        return carry

    lax.fori_loop(0, tiles, one, 0)
    lax.fori_loop(0, tiles, settle, 0)
    done.wait()


def per_device(left_block, right_block, slice_ids, mode_order):
    slices, rows_all, part_k = left_block.shape
    shard_k, values, columns = right_block.shape
    rows, width = rows_all // ROW_CHUNKS, columns // PAIRS
    bond = 4 * part_k
    late = (PAIRS - EARLY) * 2
    right = jnp.transpose(right_block, (1, 0, 2))
    vmem = pl.BlockSpec(memory_space=pltpu.VMEM)
    hbm = pl.BlockSpec(memory_space=pltpu.HBM)
    a, b, part = pl.pallas_call(
        gather_kernel,
        out_shape=(
            pltpu.VMEM((ROW_CHUNKS, 2 * rows, values * bond), jnp.bfloat16),
            pltpu.VMEM((PAIRS, 2, values, 2, 4, 4, shard_k, width // 2), jnp.bfloat16),
            pltpu.VMEM((rows_all, EARLY * width), jnp.float32),
        ),
        in_specs=[hbm, hbm, hbm, vmem],
        out_specs=(vmem, vmem, vmem),
        scratch_shapes=[
            pltpu.SMEM(slice_ids.shape, jnp.int32),
            pltpu.SMEM(mode_order.shape, jnp.int32),
            pltpu.VMEM(left_block.shape, left_block.dtype),
            pltpu.VMEM((ROW_CHUNKS, 4, values, rows + 16, part_k), jnp.int16),
            pltpu.VMEM((bond, bond), jnp.bfloat16),
            pltpu.SemaphoreType.DMA((3,)),
            pltpu.SemaphoreType.DMA((7,)),
            pltpu.SemaphoreType.DMA((2, 9, PAIRS)),
            pltpu.SemaphoreType.DMA((4, ROW_CHUNKS)),
        ],
        compiler_params=pltpu.CompilerParams(
            collective_id=0, has_side_effects=True, vmem_limit_bytes=20 << 20
        ),
    )(*(pltpu.with_memory_space_constraint(x, pltpu.HBM) for x in (slice_ids, mode_order, left_block)), right)
    return pl.pallas_call(
        finish_kernel,
        out_shape=jax.ShapeDtypeStruct((rows_all, columns), jnp.float32),
        in_specs=[vmem, vmem, vmem],
        out_specs=pl.BlockSpec(memory_space=pl.ANY),
        scratch_shapes=[
            pltpu.VMEM((late, rows_all // 2, width), jnp.float32),
            pltpu.SemaphoreType.DMA((late + 1,)),
        ],
        compiler_params=pltpu.CompilerParams(vmem_limit_bytes=20 << 20),
    )(a, b, part)


def solution(mesh):
    in_specs = (P(None, ("row", "depth"), "col"), P(("row", "depth"), None, "col"), P(), P())
    out_specs = P(("row", "depth"), "col")
    return jax.shard_map(
        per_device, mesh=mesh, in_specs=in_specs, out_specs=out_specs, check_vma=False
    )
```

```python
import functools
import math

import jax
import jax.numpy as jnp
from jax import lax
from jax.experimental import pallas as pl
from jax.experimental.pallas import tpu as pltpu
from jax.sharding import PartitionSpec as P

MESH = pl.DeviceIdType.MESH
ROW_CHUNKS = 4
PAIRS = 4
AHEAD = 1
EARLY = 3
CODE_TOP = 32000.0
STEPS_PER_OCTAVE = 16.0
LN2 = math.log(2.0)


def tile_product(a_ref, b_ref, q, p, half):
    b = b_ref[p, half]
    a = a_ref[pl.ds(2 * q, 2)]
    rows = a.shape[1] // 2
    both = jnp.dot(
        a.reshape(-1, a.shape[2]), b.reshape(-1, b.shape[-1]), preferred_element_type=jnp.float32
    )
    both = both.reshape(2, 2, rows, both.shape[1])
    return (both[:, 0] + both[:, 1]).reshape(2 * rows, both.shape[3])


def gather_kernel(
    ids_hbm,
    order_hbm,
    left_hbm,
    right_ref,
    a_ref,
    b_ref,
    part_ref,
    ids,
    order,
    left,
    code,
    pick,
    local,
    send,
    recv,
    left_recv,
):
    slices, rows_all, part_k = left.shape
    values, shard_k, columns = right_ref.shape
    rows, width = rows_all // ROW_CHUNKS, columns // PAIRS
    strip = width // 2
    bond = 4 * part_k

    row, c, y_lo = lax.axis_index("row"), lax.axis_index("col"), lax.axis_index("depth")
    core = row % 2
    y = (row // 2) % 2 * 2 + y_lo
    z = row // 4

    def place(y_at, z_at, core_at):
        return ((z_at * 2 + y_at // 2) * 2 + core_at, c, y_at % 2)

    def along_y(d):
        return place((y + d) % 4, z, core)

    def along_z(d):
        return place(y, (z + d) % 4, core)

    def along_x(d):
        return (row, (c + d) % 4, y_lo)

    sibling = place(y, z, 1 - core)

    barrier = pltpu.get_barrier_semaphore()
    for other in (along_y(1), along_y(3), along_z(1), along_z(3), along_x(1), along_x(3), sibling):
        pl.semaphore_signal(barrier, inc=1, device_id=other, device_id_type=MESH)

    staged = [
        pltpu.make_async_copy(left_hbm, left, local.at[0]),
        pltpu.make_async_copy(ids_hbm, ids, local.at[1]),
        pltpu.make_async_copy(order_hbm, order, local.at[2]),
    ]
    for one in staged:
        one.start()
    for p in range(PAIRS):
        for half in (0, 1):
            at = p * width + half * strip
            b_ref[p, half, :, core, z, y] = right_ref[:, :, at : at + strip]

    def copy(ref, signals, device):
        return pltpu.make_async_remote_copy(
            src_ref=ref,
            dst_ref=ref,
            send_sem=signals[0],
            recv_sem=signals[1],
            device_id=device,
            device_id_type=MESH,
        )

    def moved(half, kind, p):
        first, second = (along_y, along_z) if half == 0 else (along_z, along_y)
        at1, at2 = (y, z) if half == 0 else (z, y)
        both = slice(None)

        def one(v, d):
            at = (at1 + d) % 4
            where = (z, at) if half == 0 else (at, y)
            return b_ref.at[(pl.ds(p * AHEAD, AHEAD), half, v, core, *where)]

        def group(v, d):
            at = (at2 + d) % 4
            where = (at, both) if half == 0 else (both, at)
            return b_ref.at[(p, half, v, core, *where)]

        if kind == 0:
            return one(both, 0), first(1), one(both, 3)
        if kind == 1:
            return one(both, 0), first(3), one(both, 1)
        if kind == 2:
            return one(0, 3), first(1), one(0, 2)
        if kind == 3:
            return one(1, 1), first(3), one(1, 2)
        if kind == 4:
            return group(both, 0), second(1), group(both, 3)
        if kind == 5:
            return group(both, 0), second(3), group(both, 1)
        if kind == 6:
            return group(0, 3), second(1), group(0, 2)
        if kind == 7:
            return group(1, 1), second(3), group(1, 2)
        return b_ref.at[p, half, :, core], sibling, b_ref.at[p, half, :, 1 - core]

    def sems(half, kind, p):
        return send.at[kind // 2], recv.at[half, kind, p]

    def start(half, kind, p):
        ref, device, _ = moved(half, kind, p)
        copy(ref, sems(half, kind, p), device).start()

    def arrived(half, kind, p):
        copy(moved(half, kind, p)[2], sems(half, kind, p), sibling).wait_recv()

    def left_moved(kind, q):
        before, after, far = (c + 3) % 4, (c + 1) % 4, (c + 2) % 4
        if kind == 0:
            return code.at[q, c], along_x(1), code.at[q, before]
        if kind == 1:
            return code.at[q, c], along_x(3), code.at[q, after]
        if kind == 2:
            return code.at[q, before, 0], along_x(1), code.at[q, far, 0]
        return code.at[q, after, 1], along_x(3), code.at[q, far, 1]

    def left_sems(kind, q):
        return send.at[5 + kind // 2], left_recv.at[kind, q]

    def left_start(kind, q):
        ref, device, _ = left_moved(kind, q)
        copy(ref, left_sems(kind, q), device).start()

    def left_arrived(kind, q):
        copy(left_moved(kind, q)[2], left_sems(kind, q), sibling).wait_recv()

    def own_start(p):
        for half in (0, 1):
            start(half, 0, p)
            start(half, 1, p)

    def own_forward(p):
        for half in (0, 1):
            arrived(half, 0, p)
            start(half, 2, p)
            arrived(half, 1, p)
            start(half, 3, p)

    pl.semaphore_wait(barrier, 7)
    for p in range(PAIRS // AHEAD):
        own_start(p)
    for one in staged:
        one.wait()

    weights = [
        [jnp.where(ids[s] == v, 1.0, 0.0).astype(jnp.float32) for s in range(slices)]
        for v in range(values)
    ]

    def encode(q, carry):
        here = pl.ds(pl.multiple_of(q * rows, rows), rows)
        blocks = [left[s, here, :].astype(jnp.float32) for s in range(slices)]
        for v in range(values):
            total = blocks[0] * weights[v][0]
            for s in range(1, slices):
                total = total + blocks[s] * weights[v][s]
            top = jnp.max(jnp.abs(total), axis=0, keepdims=True)
            top = jnp.maximum(top, 2.0**-110)
            level = jnp.ceil(jnp.log(top) * (STEPS_PER_OCTAVE / LN2))
            scale = jnp.exp(level * (-LN2 / STEPS_PER_OCTAVE)) * CODE_TOP
            code[q, c, v, :rows, :] = jnp.round(total * scale).astype(jnp.int32).astype(jnp.int16)
            code[q, c, v, rows:, :] = jnp.broadcast_to(level, (16, part_k)).astype(jnp.int32).astype(jnp.int16)

        @pl.when(q < 2)
        def _():
            left_start(0, q)
            left_start(1, q)

        return carry

    lax.fori_loop(0, ROW_CHUNKS, encode, 0)

    place_at = lax.broadcasted_iota(jnp.int32, (8, bond), 1)
    j = place_at & 15
    at_y, at_z, plane = (place_at >> 4) & 3, (place_at >> 6) & 3, place_at >> 8
    shard = at_z * 8 + (at_y >> 1) * 4 + plane * 2 + (at_y & 1)
    logical = shard * shard_k + j
    stored = jnp.zeros((8, bond), jnp.int32)
    for bit in range(order.shape[0]):
        stored = stored + ((logical >> bit) & 1) * jnp.left_shift(jnp.int32(1), order[bit])
    hit = lax.broadcasted_iota(jnp.int32, (bond, bond), 0) == stored[:1]
    pick[...] = jnp.where(hit, 1.0, 0.0).astype(jnp.bfloat16)

    for p in range(PAIRS // AHEAD):
        own_forward(p)

    def decode(q):
        parts = []
        for v in range(values):
            high, low = [], []
            for at in range(4):
                level = code[q, at, v, rows:, :].astype(jnp.int32).astype(jnp.float32)[:1]
                scale = jnp.exp(level * (LN2 / STEPS_PER_OCTAVE)) * (1.0 / CODE_TOP)
                x = code[q, at, v, :rows, :].astype(jnp.int32).astype(jnp.float32) * scale
                h = x.astype(jnp.bfloat16)
                high.append(h)
                low.append((x - h.astype(jnp.float32)).astype(jnp.bfloat16))
            parts += [jnp.concatenate(high, axis=1), jnp.concatenate(low, axis=1)]
        picked = jnp.dot(
            jnp.concatenate(parts, axis=0), pick[...], preferred_element_type=jnp.float32
        ).astype(jnp.bfloat16)
        for v in range(values):
            a_ref[q, :, v * bond : (v + 1) * bond] = picked[2 * rows * v : 2 * rows * (v + 1)]

    def tile(q, p, half):
        at = p * width + half * strip
        part_ref[2 * q * rows : 2 * (q + 1) * rows, at : at + strip] = tile_product(a_ref, b_ref, q, p, half)

    def group_start(p):
        for half in (0, 1):
            if p % AHEAD == 0:
                arrived(half, 2, p // AHEAD)
                arrived(half, 3, p // AHEAD)
            start(half, 4, p)
            start(half, 5, p)

    def group_forward(p):
        for half in (0, 1):
            arrived(half, 4, p)
            start(half, 6, p)
            arrived(half, 5, p)
            start(half, 7, p)

    def group_last(p):
        for half in (0, 1):
            arrived(half, 6, p)
            arrived(half, 7, p)
            start(half, 8, p)

    def whole(p, half):
        arrived(half, 8, p)

    def left_forward(q):
        left_arrived(0, q)
        left_start(2, q)
        left_arrived(1, q)
        left_start(3, q)
        if q + 2 < ROW_CHUNKS:
            left_start(0, q + 2)
            left_start(1, q + 2)

    def left_whole(q):
        left_arrived(2, q)
        left_arrived(3, q)
        decode(q)

    group_start(0)
    group_start(1)
    left_forward(0)
    group_forward(0)
    group_start(2)
    left_forward(1)
    left_whole(0)
    group_forward(1)
    group_start(3)
    left_forward(2)
    group_last(0)
    left_whole(1)
    left_forward(3)
    whole(0, 0)
    tile(0, 0, 0)
    group_forward(2)
    whole(0, 1)
    tile(0, 0, 1)
    group_last(1)
    left_whole(2)
    whole(1, 0)
    tile(0, 1, 0)
    whole(1, 1)
    group_forward(3)
    tile(0, 1, 1)
    left_whole(3)
    tile(1, 0, 0)
    tile(1, 0, 1)
    group_last(2)
    tile(1, 1, 0)
    group_last(3)
    tile(1, 1, 1)
    for half in (0, 1):
        whole(2, half)
        tile(0, 2, half)
        tile(1, 2, half)
    whole(3, 0)
    whole(3, 1)

    sizes = (
        b_ref.at[0, 0, 0],
        b_ref.at[0, 0, 0, 0],
        b_ref.at[0],
        b_ref.at[0, 0],
        b_ref.at[pl.ds(0, PAIRS // 2)],
        code.at[pl.ds(0, 2)],
        code.at[0],
    )
    for n, size in enumerate(sizes):
        copy(size, (send.at[n], recv.at[0, 0, 0]), sibling).wait_send()


def finish_kernel(a_ref, b_ref, part_ref, out_ref, last, sems):
    tiles, rows, width = last.shape
    done = pltpu.make_async_copy(part_ref, out_ref.at[:, : part_ref.shape[1]], sems.at[tiles])
    done.start()

    def out_copy(n):
        here = pl.ds(pl.multiple_of(n % 2 * rows, rows), rows)
        cols = pl.ds(pl.multiple_of((n // 2 + 2 * EARLY) * width, width), width)
        return pltpu.make_async_copy(last.at[n], out_ref.at[here, cols], sems.at[n])

    def one(n, carry):
        last[n] = tile_product(a_ref, b_ref, n % 2, n // 4 + EARLY, n // 2 % 2)
        out_copy(n).start()
        return carry

    def settle(n, carry):
        out_copy(n).wait()
        return carry

    lax.fori_loop(0, tiles, one, 0)
    lax.fori_loop(0, tiles, settle, 0)
    done.wait()


def per_device(left_block, right_block, slice_ids, mode_order):
    slices, rows_all, part_k = left_block.shape
    shard_k, values, columns = right_block.shape
    rows, width = rows_all // ROW_CHUNKS, columns // PAIRS
    bond = 4 * part_k
    late = (PAIRS - EARLY) * 4
    right = jnp.transpose(right_block, (1, 0, 2))
    vmem = pl.BlockSpec(memory_space=pltpu.VMEM)
    hbm = pl.BlockSpec(memory_space=pltpu.HBM)
    a, b, part = pl.pallas_call(
        gather_kernel,
        out_shape=(
            pltpu.VMEM((ROW_CHUNKS, 2 * rows, values * bond), jnp.bfloat16),
            pltpu.VMEM((PAIRS, 2, values, 2, 4, 4, shard_k, width // 2), jnp.bfloat16),
            pltpu.VMEM((rows_all, EARLY * width), jnp.float32),
        ),
        in_specs=[hbm, hbm, hbm, vmem],
        out_specs=(vmem, vmem, vmem),
        scratch_shapes=[
            pltpu.SMEM(slice_ids.shape, jnp.int32),
            pltpu.SMEM(mode_order.shape, jnp.int32),
            pltpu.VMEM(left_block.shape, left_block.dtype),
            pltpu.VMEM((ROW_CHUNKS, 4, values, rows + 16, part_k), jnp.int16),
            pltpu.VMEM((bond, bond), jnp.bfloat16),
            pltpu.SemaphoreType.DMA((3,)),
            pltpu.SemaphoreType.DMA((7,)),
            pltpu.SemaphoreType.DMA((2, 9, PAIRS)),
            pltpu.SemaphoreType.DMA((4, ROW_CHUNKS)),
        ],
        compiler_params=pltpu.CompilerParams(
            collective_id=0, has_side_effects=True, vmem_limit_bytes=20 << 20
        ),
    )(*(pltpu.with_memory_space_constraint(x, pltpu.HBM) for x in (slice_ids, mode_order, left_block)), right)
    return pl.pallas_call(
        finish_kernel,
        out_shape=jax.ShapeDtypeStruct((rows_all, columns), jnp.float32),
        in_specs=[vmem, vmem, vmem],
        out_specs=pl.BlockSpec(memory_space=pl.ANY),
        scratch_shapes=[
            pltpu.VMEM((late, rows_all // 2, width // 2), jnp.float32),
            pltpu.SemaphoreType.DMA((late + 1,)),
        ],
        compiler_params=pltpu.CompilerParams(vmem_limit_bytes=20 << 20),
    )(a, b, part)


def solution(mesh):
    in_specs = (P(None, ("row", "depth"), "col"), P(("row", "depth"), None, "col"), P(), P())
    out_specs = P(("row", "depth"), "col")
    return jax.shard_map(
        per_device, mesh=mesh, in_specs=in_specs, out_specs=out_specs, check_vma=False
    )
```

```python
import functools
import math

import jax
import jax.numpy as jnp
from jax import lax
from jax.experimental import pallas as pl
from jax.experimental.pallas import tpu as pltpu
from jax.sharding import PartitionSpec as P

MESH = pl.DeviceIdType.MESH
ROW_CHUNKS = 4
PAIRS = 4
AHEAD = 1
EARLY = 3
CODE_TOP = 32000.0
STEPS_PER_OCTAVE = 16.0
LN2 = math.log(2.0)


def tile_product(a_ref, b_ref, q, p, half):
    b = b_ref[p, half]
    a = a_ref[pl.ds(2 * q, 2)]
    rows = a.shape[1] // 2
    both = jnp.dot(
        a.reshape(-1, a.shape[2]), b.reshape(-1, b.shape[-1]), preferred_element_type=jnp.float32
    )
    both = both.reshape(2, 2, rows, both.shape[1])
    return (both[:, 0] + both[:, 1]).reshape(2 * rows, both.shape[3])


def gather_kernel(
    ids_hbm,
    order_hbm,
    left_hbm,
    right_ref,
    a_ref,
    b_ref,
    part_ref,
    ids,
    order,
    left,
    code,
    pick,
    local,
    send,
    recv,
    left_recv,
):
    slices, rows_all, part_k = left.shape
    values, shard_k, columns = right_ref.shape
    rows, width = rows_all // ROW_CHUNKS, columns // PAIRS
    strip = width // 2
    bond = 4 * part_k

    row, c, y_lo = lax.axis_index("row"), lax.axis_index("col"), lax.axis_index("depth")
    core = row % 2
    y = (row // 2) % 2 * 2 + y_lo
    z = row // 4

    def place(y_at, z_at, core_at):
        return ((z_at * 2 + y_at // 2) * 2 + core_at, c, y_at % 2)

    def along_y(d):
        return place((y + d) % 4, z, core)

    def along_z(d):
        return place(y, (z + d) % 4, core)

    def along_x(d):
        return (row, (c + d) % 4, y_lo)

    sibling = place(y, z, 1 - core)

    barrier = pltpu.get_barrier_semaphore()
    for other in (along_y(1), along_y(3), along_z(1), along_z(3), along_x(1), along_x(3), sibling):
        pl.semaphore_signal(barrier, inc=1, device_id=other, device_id_type=MESH)

    staged = [
        pltpu.make_async_copy(left_hbm, left, local.at[0]),
        pltpu.make_async_copy(ids_hbm, ids, local.at[1]),
        pltpu.make_async_copy(order_hbm, order, local.at[2]),
    ]
    for one in staged:
        one.start()
    for p in range(PAIRS):
        for half in (0, 1):
            at = p * width + half * strip
            b_ref[p, half, :, core, z, y] = right_ref[:, :, at : at + strip]

    def copy(ref, signals, device):
        return pltpu.make_async_remote_copy(
            src_ref=ref,
            dst_ref=ref,
            send_sem=signals[0],
            recv_sem=signals[1],
            device_id=device,
            device_id_type=MESH,
        )

    def moved(half, kind, p):
        first, second = (along_y, along_z) if half == 0 else (along_z, along_y)
        at1, at2 = (y, z) if half == 0 else (z, y)
        both = slice(None)

        def one(v, d):
            at = (at1 + d) % 4
            where = (z, at) if half == 0 else (at, y)
            return b_ref.at[(pl.ds(p * AHEAD, AHEAD), half, v, core, *where)]

        def group(v, d):
            at = (at2 + d) % 4
            where = (at, both) if half == 0 else (both, at)
            return b_ref.at[(p, half, v, core, *where)]

        if kind == 0:
            return one(both, 0), first(1), one(both, 3)
        if kind == 1:
            return one(both, 0), first(3), one(both, 1)
        if kind == 2:
            return one(0, 3), first(1), one(0, 2)
        if kind == 3:
            return one(1, 1), first(3), one(1, 2)
        if kind == 4:
            return group(both, 0), second(1), group(both, 3)
        if kind == 5:
            return group(both, 0), second(3), group(both, 1)
        if kind == 6:
            return group(0, 3), second(1), group(0, 2)
        if kind == 7:
            return group(1, 1), second(3), group(1, 2)
        return b_ref.at[p, half, :, core], sibling, b_ref.at[p, half, :, 1 - core]

    def sems(half, kind, p):
        return send.at[kind // 2], recv.at[half, kind, p]

    def start(half, kind, p):
        ref, device, _ = moved(half, kind, p)
        copy(ref, sems(half, kind, p), device).start()

    def arrived(half, kind, p):
        copy(moved(half, kind, p)[2], sems(half, kind, p), sibling).wait_recv()

    def left_moved(kind, q):
        before, after, far = (c + 3) % 4, (c + 1) % 4, (c + 2) % 4
        if kind == 0:
            return code.at[q, c], along_x(1), code.at[q, before]
        if kind == 1:
            return code.at[q, c], along_x(3), code.at[q, after]
        if kind == 2:
            return code.at[q, before, 0], along_x(1), code.at[q, far, 0]
        return code.at[q, after, 1], along_x(3), code.at[q, far, 1]

    def left_sems(kind, q):
        return send.at[5 + kind // 2], left_recv.at[kind, q]

    def left_start(kind, q):
        ref, device, _ = left_moved(kind, q)
        copy(ref, left_sems(kind, q), device).start()

    def left_arrived(kind, q):
        copy(left_moved(kind, q)[2], left_sems(kind, q), sibling).wait_recv()

    def own_start(p):
        for half in (0, 1):
            start(half, 0, p)
            start(half, 1, p)

    def own_forward(p):
        for half in (0, 1):
            arrived(half, 0, p)
            start(half, 2, p)
            arrived(half, 1, p)
            start(half, 3, p)

    pl.semaphore_wait(barrier, 7)
    for p in range(PAIRS // AHEAD):
        own_start(p)
    for one in staged:
        one.wait()

    weights = [
        [jnp.where(ids[s] == v, 1.0, 0.0).astype(jnp.float32) for s in range(slices)]
        for v in range(values)
    ]

    def encode(q, carry):
        here = pl.ds(pl.multiple_of(q * rows, rows), rows)
        blocks = [left[s, here, :].astype(jnp.float32) for s in range(slices)]
        for v in range(values):
            total = blocks[0] * weights[v][0]
            for s in range(1, slices):
                total = total + blocks[s] * weights[v][s]
            top = jnp.max(jnp.abs(total), axis=0, keepdims=True)
            top = jnp.maximum(top, 2.0**-110)
            level = jnp.ceil(jnp.log(top) * (STEPS_PER_OCTAVE / LN2))
            scale = jnp.exp(level * (-LN2 / STEPS_PER_OCTAVE)) * CODE_TOP
            code[q, c, v, :rows, :] = jnp.round(total * scale).astype(jnp.int32).astype(jnp.int16)
            code[q, c, v, rows:, :] = jnp.broadcast_to(level, (16, part_k)).astype(jnp.int32).astype(jnp.int16)

        @pl.when(q < 2)
        def _():
            left_start(0, q)
            left_start(1, q)

        return carry

    lax.fori_loop(0, ROW_CHUNKS, encode, 0)

    place_at = lax.broadcasted_iota(jnp.int32, (8, bond), 1)
    j = place_at & 15
    at_y, at_z, plane = (place_at >> 4) & 3, (place_at >> 6) & 3, place_at >> 8
    shard = at_z * 8 + (at_y >> 1) * 4 + plane * 2 + (at_y & 1)
    logical = shard * shard_k + j
    stored = jnp.zeros((8, bond), jnp.int32)
    for bit in range(order.shape[0]):
        stored = stored + ((logical >> bit) & 1) * jnp.left_shift(jnp.int32(1), order[bit])
    hit = lax.broadcasted_iota(jnp.int32, (bond, bond), 0) == stored[:1]
    pick[...] = jnp.where(hit, 1.0, 0.0).astype(jnp.bfloat16)

    for p in range(PAIRS // AHEAD):
        own_forward(p)

    def decode(q):
        parts = []
        for v in range(values):
            high, low = [], []
            for at in range(4):
                level = code[q, at, v, rows:, :].astype(jnp.int32).astype(jnp.float32)[:1]
                scale = jnp.exp(level * (LN2 / STEPS_PER_OCTAVE)) * (1.0 / CODE_TOP)
                x = code[q, at, v, :rows, :].astype(jnp.int32).astype(jnp.float32) * scale
                h = x.astype(jnp.bfloat16)
                high.append(h)
                low.append((x - h.astype(jnp.float32)).astype(jnp.bfloat16))
            parts += [jnp.concatenate(high, axis=1), jnp.concatenate(low, axis=1)]
        picked = jnp.dot(
            jnp.concatenate(parts, axis=0), pick[...], preferred_element_type=jnp.float32
        ).astype(jnp.bfloat16)
        for v in range(values):
            a_ref[q, :, v * bond : (v + 1) * bond] = picked[2 * rows * v : 2 * rows * (v + 1)]

    def tile(q, p, half):
        at = p * width + half * strip
        part_ref[2 * q * rows : 2 * (q + 1) * rows, at : at + strip] = tile_product(a_ref, b_ref, q, p, half)

    def group_start(p):
        for half in (0, 1):
            if p % AHEAD == 0:
                arrived(half, 2, p // AHEAD)
                arrived(half, 3, p // AHEAD)
            start(half, 4, p)
            start(half, 5, p)

    def group_forward(p):
        for half in (0, 1):
            arrived(half, 4, p)
            start(half, 6, p)
            arrived(half, 5, p)
            start(half, 7, p)

    def group_last(p):
        for half in (0, 1):
            arrived(half, 6, p)
            arrived(half, 7, p)
            start(half, 8, p)

    def whole(p, half):
        arrived(half, 8, p)

    def left_forward(q):
        left_arrived(0, q)
        left_start(2, q)
        left_arrived(1, q)
        left_start(3, q)
        if q + 2 < ROW_CHUNKS:
            left_start(0, q + 2)
            left_start(1, q + 2)

    def left_whole(q):
        left_arrived(2, q)
        left_arrived(3, q)
        decode(q)

    group_start(0)
    group_start(1)
    left_forward(0)
    group_forward(0)
    group_start(2)
    left_forward(1)
    left_whole(0)
    group_forward(1)
    group_start(3)
    left_forward(2)
    group_last(0)
    left_whole(1)
    left_forward(3)
    whole(0, 0)
    tile(0, 0, 0)
    group_forward(2)
    whole(0, 1)
    tile(0, 0, 1)
    group_last(1)
    left_whole(2)
    left_whole(3)
    tile(1, 0, 0)
    group_forward(3)
    tile(1, 0, 1)
    whole(1, 0)
    tile(0, 1, 0)
    group_last(2)
    whole(1, 1)
    tile(0, 1, 1)
    tile(1, 1, 0)
    group_last(3)
    tile(1, 1, 1)
    for half in (0, 1):
        whole(2, half)
        tile(0, 2, half)
        tile(1, 2, half)
    whole(3, 0)
    whole(3, 1)

    sizes = (
        b_ref.at[0, 0, 0],
        b_ref.at[0, 0, 0, 0],
        b_ref.at[0],
        b_ref.at[0, 0],
        b_ref.at[pl.ds(0, PAIRS // 2)],
        code.at[pl.ds(0, 2)],
        code.at[0],
    )
    for n, size in enumerate(sizes):
        copy(size, (send.at[n], recv.at[0, 0, 0]), sibling).wait_send()


def finish_kernel(a_ref, b_ref, part_ref, out_ref, last, sems):
    tiles, rows, width = last.shape
    done = pltpu.make_async_copy(part_ref, out_ref.at[:, : part_ref.shape[1]], sems.at[tiles])
    done.start()

    def out_copy(n):
        here = pl.ds(pl.multiple_of(n % 2 * rows, rows), rows)
        cols = pl.ds(pl.multiple_of((n // 2 + 2 * EARLY) * width, width), width)
        return pltpu.make_async_copy(last.at[n], out_ref.at[here, cols], sems.at[n])

    def one(n, carry):
        last[n] = tile_product(a_ref, b_ref, n % 2, n // 4 + EARLY, n // 2 % 2)
        out_copy(n).start()
        return carry

    def settle(n, carry):
        out_copy(n).wait()
        return carry

    lax.fori_loop(0, tiles, one, 0)
    lax.fori_loop(0, tiles, settle, 0)
    done.wait()


def per_device(left_block, right_block, slice_ids, mode_order):
    slices, rows_all, part_k = left_block.shape
    shard_k, values, columns = right_block.shape
    rows, width = rows_all // ROW_CHUNKS, columns // PAIRS
    bond = 4 * part_k
    late = (PAIRS - EARLY) * 4
    right = jnp.transpose(right_block, (1, 0, 2))
    vmem = pl.BlockSpec(memory_space=pltpu.VMEM)
    hbm = pl.BlockSpec(memory_space=pltpu.HBM)
    a, b, part = pl.pallas_call(
        gather_kernel,
        out_shape=(
            pltpu.VMEM((ROW_CHUNKS, 2 * rows, values * bond), jnp.bfloat16),
            pltpu.VMEM((PAIRS, 2, values, 2, 4, 4, shard_k, width // 2), jnp.bfloat16),
            pltpu.VMEM((rows_all, EARLY * width), jnp.float32),
        ),
        in_specs=[hbm, hbm, hbm, vmem],
        out_specs=(vmem, vmem, vmem),
        scratch_shapes=[
            pltpu.SMEM(slice_ids.shape, jnp.int32),
            pltpu.SMEM(mode_order.shape, jnp.int32),
            pltpu.VMEM(left_block.shape, left_block.dtype),
            pltpu.VMEM((ROW_CHUNKS, 4, values, rows + 16, part_k), jnp.int16),
            pltpu.VMEM((bond, bond), jnp.bfloat16),
            pltpu.SemaphoreType.DMA((3,)),
            pltpu.SemaphoreType.DMA((7,)),
            pltpu.SemaphoreType.DMA((2, 9, PAIRS)),
            pltpu.SemaphoreType.DMA((4, ROW_CHUNKS)),
        ],
        compiler_params=pltpu.CompilerParams(
            collective_id=0, has_side_effects=True, vmem_limit_bytes=20 << 20
        ),
    )(*(pltpu.with_memory_space_constraint(x, pltpu.HBM) for x in (slice_ids, mode_order, left_block)), right)
    return pl.pallas_call(
        finish_kernel,
        out_shape=jax.ShapeDtypeStruct((rows_all, columns), jnp.float32),
        in_specs=[vmem, vmem, vmem],
        out_specs=pl.BlockSpec(memory_space=pl.ANY),
        scratch_shapes=[
            pltpu.VMEM((late, rows_all // 2, width // 2), jnp.float32),
            pltpu.SemaphoreType.DMA((late + 1,)),
        ],
        compiler_params=pltpu.CompilerParams(vmem_limit_bytes=20 << 20),
    )(a, b, part)


def solution(mesh):
    in_specs = (P(None, ("row", "depth"), "col"), P(("row", "depth"), None, "col"), P(), P())
    out_specs = P(("row", "depth"), "col")
    return jax.shard_map(
        per_device, mesh=mesh, in_specs=in_specs, out_specs=out_specs, check_vma=False
    )
```

```python
import functools
import math

import jax
import jax.numpy as jnp
from jax import lax
from jax.experimental import pallas as pl
from jax.experimental.pallas import tpu as pltpu
from jax.sharding import PartitionSpec as P

MESH = pl.DeviceIdType.MESH
ROW_CHUNKS = 4
PAIRS = 4
AHEAD = 1
EARLY = 3
CODE_TOP = 32000.0
STEPS_PER_OCTAVE = 16.0
LN2 = math.log(2.0)


def tile_product(a_ref, b_ref, q, p, half):
    b = b_ref[p, half]
    a = a_ref[pl.ds(2 * q, 2)]
    rows = a.shape[1] // 2
    both = jnp.dot(
        a.reshape(-1, a.shape[2]), b.reshape(-1, b.shape[-1]), preferred_element_type=jnp.float32
    )
    both = both.reshape(2, 2, rows, both.shape[1])
    return (both[:, 0] + both[:, 1]).reshape(2 * rows, both.shape[3])


def gather_kernel(
    ids_hbm,
    order_hbm,
    left_hbm,
    right_hbm,
    a_ref,
    b_ref,
    part_ref,
    ids,
    order,
    left,
    right,
    code,
    pick,
    local,
    send,
    recv,
    left_recv,
):
    slices, rows_all, part_k = left.shape
    shard_k, values, columns = right.shape
    rows, width = rows_all // ROW_CHUNKS, columns // PAIRS
    strip = width // 2
    bond = 4 * part_k

    row, c, y_lo = lax.axis_index("row"), lax.axis_index("col"), lax.axis_index("depth")
    core = row % 2
    y = (row // 2) % 2 * 2 + y_lo
    z = row // 4

    def place(y_at, z_at, core_at):
        return ((z_at * 2 + y_at // 2) * 2 + core_at, c, y_at % 2)

    def along_y(d):
        return place((y + d) % 4, z, core)

    def along_z(d):
        return place(y, (z + d) % 4, core)

    def along_x(d):
        return (row, (c + d) % 4, y_lo)

    sibling = place(y, z, 1 - core)

    barrier = pltpu.get_barrier_semaphore()
    for other in (along_y(1), along_y(3), along_z(1), along_z(3), along_x(1), along_x(3), sibling):
        pl.semaphore_signal(barrier, inc=1, device_id=other, device_id_type=MESH)

    shard = pltpu.make_async_copy(right_hbm, right, local.at[3])
    shard.start()
    staged = [
        pltpu.make_async_copy(left_hbm, left, local.at[0]),
        pltpu.make_async_copy(ids_hbm, ids, local.at[1]),
        pltpu.make_async_copy(order_hbm, order, local.at[2]),
    ]
    for one in staged:
        one.start()
    shard.wait()
    for p in range(PAIRS):
        for half in (0, 1):
            at = p * width + half * strip
            for v in range(values):
                b_ref[p, half, v, core, z, y] = right[:, v, at : at + strip]

    def copy(ref, signals, device):
        return pltpu.make_async_remote_copy(
            src_ref=ref,
            dst_ref=ref,
            send_sem=signals[0],
            recv_sem=signals[1],
            device_id=device,
            device_id_type=MESH,
        )

    def moved(half, kind, p):
        first, second = (along_y, along_z) if half == 0 else (along_z, along_y)
        at1, at2 = (y, z) if half == 0 else (z, y)
        both = slice(None)

        def one(v, d):
            at = (at1 + d) % 4
            where = (z, at) if half == 0 else (at, y)
            return b_ref.at[(pl.ds(p * AHEAD, AHEAD), half, v, core, *where)]

        def group(v, d):
            at = (at2 + d) % 4
            where = (at, both) if half == 0 else (both, at)
            return b_ref.at[(p, half, v, core, *where)]

        if kind == 0:
            return one(both, 0), first(1), one(both, 3)
        if kind == 1:
            return one(both, 0), first(3), one(both, 1)
        if kind == 2:
            return one(0, 3), first(1), one(0, 2)
        if kind == 3:
            return one(1, 1), first(3), one(1, 2)
        if kind == 4:
            return group(both, 0), second(1), group(both, 3)
        if kind == 5:
            return group(both, 0), second(3), group(both, 1)
        if kind == 6:
            return group(0, 3), second(1), group(0, 2)
        if kind == 7:
            return group(1, 1), second(3), group(1, 2)
        return b_ref.at[p, half, :, core], sibling, b_ref.at[p, half, :, 1 - core]

    def sems(half, kind, p):
        return send.at[kind // 2], recv.at[half, kind, p]

    def start(half, kind, p):
        ref, device, _ = moved(half, kind, p)
        copy(ref, sems(half, kind, p), device).start()

    def arrived(half, kind, p):
        copy(moved(half, kind, p)[2], sems(half, kind, p), sibling).wait_recv()

    def left_moved(kind, q):
        before, after, far = (c + 3) % 4, (c + 1) % 4, (c + 2) % 4
        if kind == 0:
            return code.at[q, c], along_x(1), code.at[q, before]
        if kind == 1:
            return code.at[q, c], along_x(3), code.at[q, after]
        if kind == 2:
            return code.at[q, before, 0], along_x(1), code.at[q, far, 0]
        return code.at[q, after, 1], along_x(3), code.at[q, far, 1]

    def left_sems(kind, q):
        return send.at[5 + kind // 2], left_recv.at[kind, q]

    def left_start(kind, q):
        ref, device, _ = left_moved(kind, q)
        copy(ref, left_sems(kind, q), device).start()

    def left_arrived(kind, q):
        copy(left_moved(kind, q)[2], left_sems(kind, q), sibling).wait_recv()

    def own_start(p):
        for half in (0, 1):
            start(half, 0, p)
            start(half, 1, p)

    def own_forward(p):
        for half in (0, 1):
            arrived(half, 0, p)
            start(half, 2, p)
            arrived(half, 1, p)
            start(half, 3, p)

    pl.semaphore_wait(barrier, 7)
    for p in range(PAIRS // AHEAD):
        own_start(p)
    for one in staged:
        one.wait()

    weights = [
        [jnp.where(ids[s] == v, 1.0, 0.0).astype(jnp.float32) for s in range(slices)]
        for v in range(values)
    ]

    def encode(q, carry):
        here = pl.ds(pl.multiple_of(q * rows, rows), rows)
        blocks = [left[s, here, :].astype(jnp.float32) for s in range(slices)]
        for v in range(values):
            total = blocks[0] * weights[v][0]
            for s in range(1, slices):
                total = total + blocks[s] * weights[v][s]
            top = jnp.max(jnp.abs(total), axis=0, keepdims=True)
            top = jnp.maximum(top, 2.0**-110)
            level = jnp.ceil(jnp.log(top) * (STEPS_PER_OCTAVE / LN2))
            scale = jnp.exp(level * (-LN2 / STEPS_PER_OCTAVE)) * CODE_TOP
            code[q, c, v, :rows, :] = jnp.round(total * scale).astype(jnp.int32).astype(jnp.int16)
            code[q, c, v, rows:, :] = jnp.broadcast_to(level, (16, part_k)).astype(jnp.int32).astype(jnp.int16)

        @pl.when(q < 2)
        def _():
            left_start(0, q)
            left_start(1, q)

        return carry

    lax.fori_loop(0, ROW_CHUNKS, encode, 0)

    place_at = lax.broadcasted_iota(jnp.int32, (8, bond), 1)
    j = place_at & 15
    at_y, at_z, plane = (place_at >> 4) & 3, (place_at >> 6) & 3, place_at >> 8
    origin = at_z * 8 + (at_y >> 1) * 4 + plane * 2 + (at_y & 1)
    logical = origin * shard_k + j
    stored = jnp.zeros((8, bond), jnp.int32)
    for bit in range(order.shape[0]):
        stored = stored + ((logical >> bit) & 1) * jnp.left_shift(jnp.int32(1), order[bit])
    hit = lax.broadcasted_iota(jnp.int32, (bond, bond), 0) == stored[:1]
    pick[...] = jnp.where(hit, 1.0, 0.0).astype(jnp.bfloat16)

    for p in range(PAIRS // AHEAD):
        own_forward(p)

    def decode(q):
        parts = []
        for v in range(values):
            high, low = [], []
            for at in range(4):
                level = code[q, at, v, rows:, :].astype(jnp.int32).astype(jnp.float32)[:1]
                scale = jnp.exp(level * (LN2 / STEPS_PER_OCTAVE)) * (1.0 / CODE_TOP)
                x = code[q, at, v, :rows, :].astype(jnp.int32).astype(jnp.float32) * scale
                h = x.astype(jnp.bfloat16)
                high.append(h)
                low.append((x - h.astype(jnp.float32)).astype(jnp.bfloat16))
            parts += [jnp.concatenate(high, axis=1), jnp.concatenate(low, axis=1)]
        picked = jnp.dot(
            jnp.concatenate(parts, axis=0), pick[...], preferred_element_type=jnp.float32
        ).astype(jnp.bfloat16)
        for v in range(values):
            a_ref[q, :, v * bond : (v + 1) * bond] = picked[2 * rows * v : 2 * rows * (v + 1)]

    def tile(q, p, half):
        at = p * width + half * strip
        part_ref[2 * q * rows : 2 * (q + 1) * rows, at : at + strip] = tile_product(a_ref, b_ref, q, p, half)

    def group_start(p):
        for half in (0, 1):
            if p % AHEAD == 0:
                arrived(half, 2, p // AHEAD)
                arrived(half, 3, p // AHEAD)
            start(half, 4, p)
            start(half, 5, p)

    def group_forward(p):
        for half in (0, 1):
            arrived(half, 4, p)
            start(half, 6, p)
            arrived(half, 5, p)
            start(half, 7, p)

    def group_last(p):
        for half in (0, 1):
            arrived(half, 6, p)
            arrived(half, 7, p)
            start(half, 8, p)

    def whole(p, half):
        arrived(half, 8, p)

    def left_forward(q):
        left_arrived(0, q)
        left_start(2, q)
        left_arrived(1, q)
        left_start(3, q)
        if q + 2 < ROW_CHUNKS:
            left_start(0, q + 2)
            left_start(1, q + 2)

    def left_whole(q):
        left_arrived(2, q)
        left_arrived(3, q)
        decode(q)

    group_start(0)
    group_start(1)
    left_forward(0)
    group_forward(0)
    group_start(2)
    left_forward(1)
    left_whole(0)
    group_forward(1)
    group_start(3)
    left_forward(2)
    group_last(0)
    left_whole(1)
    left_forward(3)
    whole(0, 0)
    tile(0, 0, 0)
    group_forward(2)
    whole(0, 1)
    tile(0, 0, 1)
    group_last(1)
    left_whole(2)
    left_whole(3)
    tile(1, 0, 0)
    group_forward(3)
    tile(1, 0, 1)
    whole(1, 0)
    tile(0, 1, 0)
    group_last(2)
    whole(1, 1)
    tile(0, 1, 1)
    tile(1, 1, 0)
    group_last(3)
    tile(1, 1, 1)
    for half in (0, 1):
        whole(2, half)
        tile(0, 2, half)
        tile(1, 2, half)
    whole(3, 0)
    whole(3, 1)

    sizes = (
        b_ref.at[0, 0, 0],
        b_ref.at[0, 0, 0, 0],
        b_ref.at[0],
        b_ref.at[0, 0],
        b_ref.at[pl.ds(0, PAIRS // 2)],
        code.at[pl.ds(0, 2)],
        code.at[0],
    )
    for n, size in enumerate(sizes):
        copy(size, (send.at[n], recv.at[0, 0, 0]), sibling).wait_send()


def finish_kernel(a_ref, b_ref, part_ref, out_ref, last, sems):
    tiles, rows, width = last.shape
    done = pltpu.make_async_copy(part_ref, out_ref.at[:, : part_ref.shape[1]], sems.at[tiles])
    done.start()

    def out_copy(n):
        here = pl.ds(pl.multiple_of(n % 2 * rows, rows), rows)
        cols = pl.ds(pl.multiple_of((n // 2 + 2 * EARLY) * width, width), width)
        return pltpu.make_async_copy(last.at[n], out_ref.at[here, cols], sems.at[n])

    def one(n, carry):
        last[n] = tile_product(a_ref, b_ref, n % 2, n // 4 + EARLY, n // 2 % 2)
        out_copy(n).start()
        return carry

    def settle(n, carry):
        out_copy(n).wait()
        return carry

    lax.fori_loop(0, tiles, one, 0)
    lax.fori_loop(0, tiles, settle, 0)
    done.wait()


def per_device(left_block, right_block, slice_ids, mode_order):
    slices, rows_all, part_k = left_block.shape
    shard_k, values, columns = right_block.shape
    rows, width = rows_all // ROW_CHUNKS, columns // PAIRS
    bond = 4 * part_k
    late = (PAIRS - EARLY) * 4
    vmem = pl.BlockSpec(memory_space=pltpu.VMEM)
    hbm = pl.BlockSpec(memory_space=pltpu.HBM)
    a, b, part = pl.pallas_call(
        gather_kernel,
        out_shape=(
            pltpu.VMEM((ROW_CHUNKS, 2 * rows, values * bond), jnp.bfloat16),
            pltpu.VMEM((PAIRS, 2, values, 2, 4, 4, shard_k, width // 2), jnp.bfloat16),
            pltpu.VMEM((rows_all, EARLY * width), jnp.float32),
        ),
        in_specs=[hbm, hbm, hbm, hbm],
        out_specs=(vmem, vmem, vmem),
        scratch_shapes=[
            pltpu.SMEM(slice_ids.shape, jnp.int32),
            pltpu.SMEM(mode_order.shape, jnp.int32),
            pltpu.VMEM(left_block.shape, left_block.dtype),
            pltpu.VMEM(right_block.shape, right_block.dtype),
            pltpu.VMEM((ROW_CHUNKS, 4, values, rows + 16, part_k), jnp.int16),
            pltpu.VMEM((bond, bond), jnp.bfloat16),
            pltpu.SemaphoreType.DMA((4,)),
            pltpu.SemaphoreType.DMA((7,)),
            pltpu.SemaphoreType.DMA((2, 9, PAIRS)),
            pltpu.SemaphoreType.DMA((4, ROW_CHUNKS)),
        ],
        compiler_params=pltpu.CompilerParams(
            collective_id=0, has_side_effects=True, vmem_limit_bytes=20 << 20
        ),
    )(*(pltpu.with_memory_space_constraint(x, pltpu.HBM) for x in (slice_ids, mode_order, left_block, right_block)))
    return pl.pallas_call(
        finish_kernel,
        out_shape=jax.ShapeDtypeStruct((rows_all, columns), jnp.float32),
        in_specs=[vmem, vmem, vmem],
        out_specs=pl.BlockSpec(memory_space=pl.ANY),
        scratch_shapes=[
            pltpu.VMEM((late, rows_all // 2, width // 2), jnp.float32),
            pltpu.SemaphoreType.DMA((late + 1,)),
        ],
        compiler_params=pltpu.CompilerParams(vmem_limit_bytes=20 << 20),
    )(a, b, part)


def solution(mesh):
    in_specs = (P(None, ("row", "depth"), "col"), P(("row", "depth"), None, "col"), P(), P())
    out_specs = P(("row", "depth"), "col")
    return jax.shard_map(
        per_device, mesh=mesh, in_specs=in_specs, out_specs=out_specs, check_vma=False
    )
```

```python
import functools
import math

import jax
import jax.numpy as jnp
from jax import lax
from jax.experimental import pallas as pl
from jax.experimental.pallas import tpu as pltpu
from jax.sharding import PartitionSpec as P

MESH = pl.DeviceIdType.MESH
ROW_CHUNKS = 4
PAIRS = 4
AHEAD = 1
EARLY = 5
CODE_TOP = 32000.0
STEPS_PER_OCTAVE = 16.0
LN2 = math.log(2.0)


def tile_product(a_ref, b_ref, q, p, half):
    b = b_ref[p, half]
    a = a_ref[pl.ds(2 * q, 2)]
    rows = a.shape[1] // 2
    both = jnp.dot(
        a.reshape(-1, a.shape[2]), b.reshape(-1, b.shape[-1]), preferred_element_type=jnp.float32
    )
    both = both.reshape(2, 2, rows, both.shape[1])
    return (both[:, 0] + both[:, 1]).reshape(2 * rows, both.shape[3])


def gather_kernel(
    ids_hbm,
    order_hbm,
    left_hbm,
    right_hbm,
    a_ref,
    b_ref,
    part_ref,
    ids,
    order,
    left,
    right,
    code,
    pick,
    local,
    send,
    recv,
    left_recv,
):
    slices, rows_all, part_k = left.shape
    shard_k, values, columns = right.shape
    rows, width = rows_all // ROW_CHUNKS, columns // PAIRS
    strip = width // 2
    bond = 4 * part_k

    row, c, y_lo = lax.axis_index("row"), lax.axis_index("col"), lax.axis_index("depth")
    core = row % 2
    y = (row // 2) % 2 * 2 + y_lo
    z = row // 4

    def place(y_at, z_at, core_at):
        return ((z_at * 2 + y_at // 2) * 2 + core_at, c, y_at % 2)

    def along_y(d):
        return place((y + d) % 4, z, core)

    def along_z(d):
        return place(y, (z + d) % 4, core)

    def along_x(d):
        return (row, (c + d) % 4, y_lo)

    sibling = place(y, z, 1 - core)

    barrier = pltpu.get_barrier_semaphore()
    for other in (along_y(1), along_y(3), along_z(1), along_z(3), along_x(1), along_x(3), sibling):
        pl.semaphore_signal(barrier, inc=1, device_id=other, device_id_type=MESH)

    shard = pltpu.make_async_copy(right_hbm, right, local.at[3])
    shard.start()
    staged = [
        pltpu.make_async_copy(left_hbm, left, local.at[0]),
        pltpu.make_async_copy(ids_hbm, ids, local.at[1]),
        pltpu.make_async_copy(order_hbm, order, local.at[2]),
    ]
    for one in staged:
        one.start()
    shard.wait()
    for p in range(PAIRS):
        for half in (0, 1):
            at = p * width + half * strip
            for v in range(values):
                b_ref[p, half, v, core, z, y] = right[:, v, at : at + strip]

    def copy(ref, signals, device):
        return pltpu.make_async_remote_copy(
            src_ref=ref,
            dst_ref=ref,
            send_sem=signals[0],
            recv_sem=signals[1],
            device_id=device,
            device_id_type=MESH,
        )

    def moved(half, kind, p):
        first, second = (along_y, along_z) if half == 0 else (along_z, along_y)
        at1, at2 = (y, z) if half == 0 else (z, y)
        both = slice(None)

        def one(v, d):
            at = (at1 + d) % 4
            where = (z, at) if half == 0 else (at, y)
            return b_ref.at[(pl.ds(p * AHEAD, AHEAD), half, v, core, *where)]

        def group(v, d):
            at = (at2 + d) % 4
            where = (at, both) if half == 0 else (both, at)
            return b_ref.at[(p, half, v, core, *where)]

        if kind == 0:
            return one(both, 0), first(1), one(both, 3)
        if kind == 1:
            return one(both, 0), first(3), one(both, 1)
        if kind == 2:
            return one(0, 3), first(1), one(0, 2)
        if kind == 3:
            return one(1, 1), first(3), one(1, 2)
        if kind == 4:
            return group(both, 0), second(1), group(both, 3)
        if kind == 5:
            return group(both, 0), second(3), group(both, 1)
        if kind == 6:
            return group(0, 3), second(1), group(0, 2)
        if kind == 7:
            return group(1, 1), second(3), group(1, 2)
        return b_ref.at[p, half, :, core], sibling, b_ref.at[p, half, :, 1 - core]

    def sems(half, kind, p):
        return send.at[kind // 2], recv.at[half, kind, p]

    def start(half, kind, p):
        ref, device, _ = moved(half, kind, p)
        copy(ref, sems(half, kind, p), device).start()

    def arrived(half, kind, p):
        copy(moved(half, kind, p)[2], sems(half, kind, p), sibling).wait_recv()

    def left_moved(kind, q):
        before, after, far = (c + 3) % 4, (c + 1) % 4, (c + 2) % 4
        if kind == 0:
            return code.at[q, c], along_x(1), code.at[q, before]
        if kind == 1:
            return code.at[q, c], along_x(3), code.at[q, after]
        if kind == 2:
            return code.at[q, before, 0], along_x(1), code.at[q, far, 0]
        return code.at[q, after, 1], along_x(3), code.at[q, far, 1]

    def left_sems(kind, q):
        return send.at[5 + kind // 2], left_recv.at[kind, q]

    def left_start(kind, q):
        ref, device, _ = left_moved(kind, q)
        copy(ref, left_sems(kind, q), device).start()

    def left_arrived(kind, q):
        copy(left_moved(kind, q)[2], left_sems(kind, q), sibling).wait_recv()

    def own_start(p):
        for half in (0, 1):
            start(half, 0, p)
            start(half, 1, p)

    def own_forward(p):
        for half in (0, 1):
            arrived(half, 0, p)
            start(half, 2, p)
            arrived(half, 1, p)
            start(half, 3, p)

    pl.semaphore_wait(barrier, 7)
    for p in range(PAIRS // AHEAD):
        own_start(p)
    for one in staged:
        one.wait()

    weights = [
        [jnp.where(ids[s] == v, 1.0, 0.0).astype(jnp.float32) for s in range(slices)]
        for v in range(values)
    ]

    def encode(q, carry):
        here = pl.ds(pl.multiple_of(q * rows, rows), rows)
        blocks = [left[s, here, :].astype(jnp.float32) for s in range(slices)]
        for v in range(values):
            total = blocks[0] * weights[v][0]
            for s in range(1, slices):
                total = total + blocks[s] * weights[v][s]
            top = jnp.max(jnp.abs(total), axis=0, keepdims=True)
            top = jnp.maximum(top, 2.0**-110)
            level = jnp.ceil(jnp.log(top) * (STEPS_PER_OCTAVE / LN2))
            scale = jnp.exp(level * (-LN2 / STEPS_PER_OCTAVE)) * CODE_TOP
            code[q, c, v, :rows, :] = jnp.round(total * scale).astype(jnp.int32).astype(jnp.int16)
            code[q, c, v, rows:, :] = jnp.broadcast_to(level, (16, part_k)).astype(jnp.int32).astype(jnp.int16)

        @pl.when(q < 2)
        def _():
            left_start(0, q)
            left_start(1, q)

        return carry

    lax.fori_loop(0, ROW_CHUNKS, encode, 0)

    place_at = lax.broadcasted_iota(jnp.int32, (8, bond), 1)
    j = place_at & 15
    at_y, at_z, plane = (place_at >> 4) & 3, (place_at >> 6) & 3, place_at >> 8
    origin = at_z * 8 + (at_y >> 1) * 4 + plane * 2 + (at_y & 1)
    logical = origin * shard_k + j
    stored = jnp.zeros((8, bond), jnp.int32)
    for bit in range(order.shape[0]):
        stored = stored + ((logical >> bit) & 1) * jnp.left_shift(jnp.int32(1), order[bit])
    hit = lax.broadcasted_iota(jnp.int32, (bond, bond), 0) == stored[:1]
    pick[...] = jnp.where(hit, 1.0, 0.0).astype(jnp.bfloat16)

    for p in range(PAIRS // AHEAD):
        own_forward(p)

    def decode(q):
        parts = []
        for v in range(values):
            high, low = [], []
            for at in range(4):
                level = code[q, at, v, rows:, :].astype(jnp.int32).astype(jnp.float32)[:1]
                scale = jnp.exp(level * (LN2 / STEPS_PER_OCTAVE)) * (1.0 / CODE_TOP)
                x = code[q, at, v, :rows, :].astype(jnp.int32).astype(jnp.float32) * scale
                h = x.astype(jnp.bfloat16)
                high.append(h)
                low.append((x - h.astype(jnp.float32)).astype(jnp.bfloat16))
            parts += [jnp.concatenate(high, axis=1), jnp.concatenate(low, axis=1)]
        picked = jnp.dot(
            jnp.concatenate(parts, axis=0), pick[...], preferred_element_type=jnp.float32
        ).astype(jnp.bfloat16)
        for v in range(values):
            a_ref[q, :, v * bond : (v + 1) * bond] = picked[2 * rows * v : 2 * rows * (v + 1)]

    def tile(q, p, half):
        at = p * width + half * strip
        part_ref[2 * q * rows : 2 * (q + 1) * rows, at : at + strip] = tile_product(a_ref, b_ref, q, p, half)

    def group_start(p):
        for half in (0, 1):
            if p % AHEAD == 0:
                arrived(half, 2, p // AHEAD)
                arrived(half, 3, p // AHEAD)
            start(half, 4, p)
            start(half, 5, p)

    def group_forward(p):
        for half in (0, 1):
            arrived(half, 4, p)
            start(half, 6, p)
            arrived(half, 5, p)
            start(half, 7, p)

    def group_last(p):
        for half in (0, 1):
            arrived(half, 6, p)
            arrived(half, 7, p)
            start(half, 8, p)

    def whole(p, half):
        arrived(half, 8, p)

    def left_forward(q):
        left_arrived(0, q)
        left_start(2, q)
        left_arrived(1, q)
        left_start(3, q)
        if q + 2 < ROW_CHUNKS:
            left_start(0, q + 2)
            left_start(1, q + 2)

    def left_whole(q):
        left_arrived(2, q)
        left_arrived(3, q)
        decode(q)

    group_start(0)
    group_start(1)
    left_forward(0)
    group_forward(0)
    group_start(2)
    left_forward(1)
    left_whole(0)
    group_forward(1)
    group_start(3)
    left_forward(2)
    group_last(0)
    left_whole(1)
    left_forward(3)
    whole(0, 0)
    tile(0, 0, 0)
    group_forward(2)
    whole(0, 1)
    tile(0, 0, 1)
    group_last(1)
    left_whole(2)
    left_whole(3)
    group_forward(3)
    tile(1, 0, 0)
    whole(1, 0)
    tile(1, 0, 1)
    tile(0, 1, 0)
    group_last(2)
    whole(1, 1)
    tile(0, 1, 1)
    tile(1, 1, 0)
    group_last(3)
    tile(1, 1, 1)
    whole(2, 0)
    tile(0, 2, 0)
    tile(1, 2, 0)
    whole(2, 1)
    whole(3, 0)
    whole(3, 1)

    sizes = (
        b_ref.at[0, 0, 0],
        b_ref.at[0, 0, 0, 0],
        b_ref.at[0],
        b_ref.at[0, 0],
        b_ref.at[pl.ds(0, PAIRS // 2)],
        code.at[pl.ds(0, 2)],
        code.at[0],
    )
    for n, size in enumerate(sizes):
        copy(size, (send.at[n], recv.at[0, 0, 0]), sibling).wait_send()


def finish_kernel(a_ref, b_ref, part_ref, out_ref, last, sems):
    tiles, rows, width = last.shape
    done = pltpu.make_async_copy(part_ref, out_ref.at[:, : part_ref.shape[1]], sems.at[tiles])
    done.start()

    def out_copy(n):
        here = pl.ds(pl.multiple_of(n % 2 * rows, rows), rows)
        cols = pl.ds(pl.multiple_of((n // 2 + EARLY) * width, width), width)
        return pltpu.make_async_copy(last.at[n], out_ref.at[here, cols], sems.at[n])

    def one(n, carry):
        last[n] = tile_product(a_ref, b_ref, n % 2, (n // 2 + EARLY) // 2, (n // 2 + EARLY) % 2)
        out_copy(n).start()
        return carry

    def settle(n, carry):
        out_copy(n).wait()
        return carry

    lax.fori_loop(0, tiles, one, 0)
    lax.fori_loop(0, tiles, settle, 0)
    done.wait()


def per_device(left_block, right_block, slice_ids, mode_order):
    slices, rows_all, part_k = left_block.shape
    shard_k, values, columns = right_block.shape
    rows, width = rows_all // ROW_CHUNKS, columns // PAIRS
    bond = 4 * part_k
    late = (2 * PAIRS - EARLY) * 2
    vmem = pl.BlockSpec(memory_space=pltpu.VMEM)
    hbm = pl.BlockSpec(memory_space=pltpu.HBM)
    a, b, part = pl.pallas_call(
        gather_kernel,
        out_shape=(
            pltpu.VMEM((ROW_CHUNKS, 2 * rows, values * bond), jnp.bfloat16),
            pltpu.VMEM((PAIRS, 2, values, 2, 4, 4, shard_k, width // 2), jnp.bfloat16),
            pltpu.VMEM((rows_all, EARLY * width // 2), jnp.float32),
        ),
        in_specs=[hbm, hbm, hbm, hbm],
        out_specs=(vmem, vmem, vmem),
        scratch_shapes=[
            pltpu.SMEM(slice_ids.shape, jnp.int32),
            pltpu.SMEM(mode_order.shape, jnp.int32),
            pltpu.VMEM(left_block.shape, left_block.dtype),
            pltpu.VMEM(right_block.shape, right_block.dtype),
            pltpu.VMEM((ROW_CHUNKS, 4, values, rows + 16, part_k), jnp.int16),
            pltpu.VMEM((bond, bond), jnp.bfloat16),
            pltpu.SemaphoreType.DMA((4,)),
            pltpu.SemaphoreType.DMA((7,)),
            pltpu.SemaphoreType.DMA((2, 9, PAIRS)),
            pltpu.SemaphoreType.DMA((4, ROW_CHUNKS)),
        ],
        compiler_params=pltpu.CompilerParams(
            collective_id=0, has_side_effects=True, vmem_limit_bytes=20 << 20
        ),
    )(*(pltpu.with_memory_space_constraint(x, pltpu.HBM) for x in (slice_ids, mode_order, left_block, right_block)))
    return pl.pallas_call(
        finish_kernel,
        out_shape=jax.ShapeDtypeStruct((rows_all, columns), jnp.float32),
        in_specs=[vmem, vmem, vmem],
        out_specs=pl.BlockSpec(memory_space=pl.ANY),
        scratch_shapes=[
            pltpu.VMEM((late, rows_all // 2, width // 2), jnp.float32),
            pltpu.SemaphoreType.DMA((late + 1,)),
        ],
        compiler_params=pltpu.CompilerParams(vmem_limit_bytes=20 << 20),
    )(a, b, part)


def solution(mesh):
    in_specs = (P(None, ("row", "depth"), "col"), P(("row", "depth"), None, "col"), P(), P())
    out_specs = P(("row", "depth"), "col")
    return jax.shard_map(
        per_device, mesh=mesh, in_specs=in_specs, out_specs=out_specs, check_vma=False
    )
```
